512 devices in a mesh: region: 16 (over z, core), pos: 32 (over x, y).
Axes of the slice: x: 4, y: 8, z: 8, core: 2. Of those that a mesh axis runs over, the one named last changes fastest.
Arguments:
- object_tiles: bfloat16 [2, 2048, 4096], P(None, 'region', 'pos'), may hold values from -4.1875 to 4.1875
- probe: float32 [2, 4, 128, 128], replicated, may hold values from -3 to 3
- amplitudes: float32 [16, 128, 128, 128], P('region', 'pos'), may hold values from 0.3 to 6
- offsets: int32 [16, 2, 128], P('region', None, 'pos'), may hold values from 0 to 127
- counts: int32 [16, 32], P('region', 'pos'), may hold values from 1 to 4
Outputs:
- object_grad: float32 [2, 2048, 4096], P(None, 'region', 'pos')
- probe_grad: float32 [2, 4, 128, 128], replicated
The draws below stay inside these ranges and needn't reach their ends.
All inputs are finite; a program needn't handle non-finite values.
Results may differ from the reference program's by a relative error of at most 0.0003.
Values may be sent and summed in bfloat16 or wider, within the bound.
A program may use at most 64 MiB of HBM per device.

```python
import math
import jax
import jax.numpy as jnp
from jax import lax

DETECTOR_PIXELS = 128
MODES = 4
P_CAP = 4
OROWS = 2048
OCOLS = 4096
STRIP_SLOTS = 128
N_REGION = 16
N_POS = 32


def set_ends(values, own_key, smallest, top_value):
    place = [jax.random.randint(jax.random.fold_in(own_key, axis), (), 0, length) for axis, length in enumerate(values.shape)]
    main_axis = values.shape.index(max(values.shape))
    next_to = place[:main_axis] + [(place[main_axis] + 1) % values.shape[main_axis]] + place[main_axis + 1:]
    return values.at[tuple(place)].set(smallest).at[tuple(next_to)].set(top_value)


def level_of(rng, dims, split, smallest, high):
    factor_of = 1.0
    for dim, shards_of in split:
        draws = jax.random.uniform(jax.random.fold_in(jax.random.fold_in(rng, 6), dim), (shards_of,), jnp.float32, smallest / len(split), high / len(split))
        factor_of = factor_of * jnp.repeat(jnp.exp(draws), dims[dim] // shards_of).reshape((-1,) + (1,) * (len(dims) - 1 - dim))
    return factor_of


def bell_draw(stream_key, shape, deviation, reach, pieces=(), kind=jnp.bfloat16):
    loudness = level_of(stream_key, shape, pieces, -0.22, 0.18) if pieces else 1.0
    entries = jax.random.normal(stream_key, shape, jnp.float32) * deviation * loudness
    return jnp.minimum(jnp.maximum(entries, -reach), reach).astype(kind)


def setup_inputs(seed: int = 0) -> dict:
    key_list = jax.random.split(jax.random.key(seed), 6)
    return {
        "object_tiles": bell_draw(key_list[0], (2, OROWS, OCOLS), 0.7, 4.1875, ((1, 16), (2, 32))),
        "probe": bell_draw(key_list[1], (2, MODES, DETECTOR_PIXELS, DETECTOR_PIXELS), 0.5, 3.0, (), jnp.float32),
        "amplitudes": jnp.clip(jnp.exp(math.log(6.0) - 2.9957322 * jax.random.uniform(key_list[2], (N_REGION, STRIP_SLOTS, DETECTOR_PIXELS, DETECTOR_PIXELS), jnp.float32) ** level_of(key_list[2], (N_REGION, STRIP_SLOTS, DETECTOR_PIXELS, DETECTOR_PIXELS), ((0, 16), (1, 32)), -0.2, 0.2)), 0.3, 6.0),
        "offsets": set_ends(jax.random.randint(key_list[3], (N_REGION, 2, STRIP_SLOTS), 0, DETECTOR_PIXELS), jax.random.fold_in(key_list[3], 1), 0, DETECTOR_PIXELS - 1).astype(jnp.int32),
        "counts": set_ends(jax.random.randint(key_list[4], (N_REGION, N_POS), 1, P_CAP + 1), jax.random.fold_in(key_list[4], 1), 1, P_CAP).astype(jnp.int32),
    }


def dft_tables(order):
    row_index_list = jnp.arange(order, dtype=jnp.int32)
    product = row_index_list[:, None] * row_index_list[None, :] % order
    angle = product.astype(jnp.float32) * (2.0 * math.pi / order)
    norm_factor = 1.0 / math.sqrt(order)
    return (jnp.cos(angle) * norm_factor, jnp.sin(angle) * norm_factor)

def both_sides(real_part, imag_part, cos_table, sin_table):
    high = lax.Precision.HIGHEST
    left_r = jnp.einsum('ab,mbc->mac', cos_table, real_part, precision=high) - jnp.einsum('ab,mbc->mac', sin_table, imag_part, precision=high)
    left_i = jnp.einsum('ab,mbc->mac', cos_table, imag_part, precision=high) + jnp.einsum('ab,mbc->mac', sin_table, real_part, precision=high)
    right_r = jnp.einsum('mab,bc->mac', left_r, cos_table, precision=high) - jnp.einsum('mab,bc->mac', left_i, sin_table, precision=high)
    right_i = jnp.einsum('mab,bc->mac', left_i, cos_table, precision=high) + jnp.einsum('mab,bc->mac', left_r, sin_table, precision=high)
    return (right_r, right_i)

def position_terms(obj_patch, probe, amplitude, cos_table, sin_table):
    exit_r = probe[0] * obj_patch[0][None] - probe[1] * obj_patch[1][None]
    exit_i = probe[0] * obj_patch[1][None] + probe[1] * obj_patch[0][None]
    far_r, far_i = both_sides(exit_r, exit_i, cos_table, -sin_table)
    intensity = lax.optimization_barrier(jnp.sum(far_r * far_r + far_i * far_i, axis=0))
    factor = 1.0 - amplitude / jnp.sqrt(intensity + 1.0)
    back_r, back_i = both_sides(far_r * factor[None], far_i * factor[None], cos_table, sin_table)
    obj_r = lax.optimization_barrier(jnp.sum(probe[0] * back_r + probe[1] * back_i, axis=0))
    obj_i = lax.optimization_barrier(jnp.sum(probe[0] * back_i - probe[1] * back_r, axis=0))
    probe_r = obj_patch[0][None] * back_r + obj_patch[1][None] * back_i
    probe_i = obj_patch[0][None] * back_i - obj_patch[1][None] * back_r
    return (jnp.stack([obj_r, obj_i]), jnp.stack([probe_r, probe_i]))

def reference(object_tiles, probe, amplitudes, offsets, counts):
    cos_table, sin_table = dft_tables(DETECTOR_PIXELS)
    field = jnp.pad(object_tiles.astype(jnp.float32), ((0, 0), (0, DETECTOR_PIXELS), (0, DETECTOR_PIXELS)))
    slot_ids = jnp.arange(N_POS * P_CAP, dtype=jnp.int32)
    region_ids = jnp.arange(N_REGION, dtype=jnp.int32)
    tile_cols = (slot_ids // P_CAP).astype(jnp.int32)
    row_start = (offsets[:, 0, :] + region_ids[:, None] * DETECTOR_PIXELS).astype(jnp.int32).reshape(-1)
    column_begin = (offsets[:, 1, :] + tile_cols[None, :] * DETECTOR_PIXELS).astype(jnp.int32).reshape(-1)
    live_flag = ((slot_ids % P_CAP)[None, :] < counts[:, tile_cols]).astype(jnp.float32).reshape(-1)
    flat_amp = amplitudes.reshape(-1, DETECTOR_PIXELS, DETECTOR_PIXELS)
    zero_index = jnp.zeros((), jnp.int32)

    def visit(carry, item):
        grad_field, probe_sum = carry
        row0, col0, amplitude, weight = item
        obj_patch = lax.dynamic_slice(field, (zero_index, row0, col0), (2, DETECTOR_PIXELS, DETECTOR_PIXELS))
        obj_term, probe_term = position_terms(obj_patch, probe, amplitude, cos_table, sin_table)
        current = lax.dynamic_slice(grad_field, (zero_index, row0, col0), (2, DETECTOR_PIXELS, DETECTOR_PIXELS))
        grad_field = lax.dynamic_update_slice(grad_field, current + weight * obj_term, (zero_index, row0, col0))
        return ((grad_field, probe_sum + weight * probe_term), None)
    start = (jnp.zeros(field.shape, jnp.float32), jnp.zeros(probe.shape, jnp.float32))
    (grad_field, probe_sum), ignored_value = lax.scan(visit, start, (row_start, column_begin, flat_amp, live_flag))
    scale = 1.0 / math.sqrt(N_REGION * N_POS * P_CAP)
    return (grad_field[:, :OROWS, :OCOLS], probe_sum * scale)
```

```python
import functools
import math

import jax
import jax.numpy as jnp
import numpy as np
from jax import lax
from jax.experimental import pallas as pl
from jax.experimental.pallas import tpu as pltpu
from jax.sharding import PartitionSpec as P

MESH = pl.DeviceIdType.MESH
F32 = jnp.float32
BF16 = jnp.bfloat16
CHUNKS = 2


def dft_parts(order):
    index = np.arange(order)
    angle = (index[:, None] * index[None, :] % order) * (2.0 * math.pi / order)
    cos, sin = np.cos(angle) / math.sqrt(order), np.sin(angle) / math.sqrt(order)
    right = np.block([[cos, -sin], [sin, cos]]).astype(np.float32)
    parts = []
    for table in (right, right.T):
        high = table.astype(jnp.bfloat16)
        low = (table - high.astype(np.float32)).astype(jnp.bfloat16)
        parts.append(np.stack([high, low]))
    return np.stack(parts)


def split(value):
    high = value.astype(BF16)
    return high, (value - high.astype(F32)).astype(BF16)


def dot(a, b):
    return jnp.dot(a, b, preferred_element_type=F32)


def on_left(table, value):
    high, low = value
    return dot(
        jnp.concatenate([table[0], table[0], table[1]], axis=1),
        jnp.concatenate([high, low, high], axis=0),
    )


def on_right(value, table):
    high, low = value
    return dot(
        jnp.concatenate([high, low, high], axis=1),
        jnp.concatenate([table[0], table[0], table[1]], axis=0),
    )


def one_hot(shape, dim, shift, limit=None):
    along = lax.broadcasted_iota(jnp.int32, shape, dim)
    other = lax.broadcasted_iota(jnp.int32, shape, 1 - dim)
    hit = along == other + shift
    if limit is not None:
        hit = jnp.logical_and(hit, along < limit)
    return jnp.where(hit, 1.0, 0.0).astype(BF16)


def kernel(
    sizes, scale, tile, probe_h, amp_h, offsets, counts, tables_h, obj_out, probe_out,
    window, probe, amp, tables, crops, res_high, res_low, obj_terms, grads, terms, own, from_core, by_x, from_x, by_y,
    from_y, by_z, from_grad, load_sem, halo_send, halo_recv, grad_send, grad_recv, core_send, core_recv,
    x_send, x_recv, y_send, y_recv, z_send, z_recv, gy_send, gy_recv, gx_send, gx_recv, gc_send, gc_recv,
):
    nx, ny, nz, slots, modes, edge = sizes
    region, pos = lax.axis_index("region"), lax.axis_index("pos")
    n_region, n_pos = 2 * nz, nx * ny
    z, core = region // 2, lax.rem(region, 2)
    x, y = pos // ny, lax.rem(pos, ny)
    up, down = lax.rem(region + n_region - 1, n_region), lax.rem(region + 1, n_region)
    left, right = lax.rem(pos + n_pos - 1, n_pos), lax.rem(pos + 1, n_pos)
    sibling = (region + 1 - 2 * core, pos)

    def at_x(step):
        return (region, lax.rem(x + step, nx) * ny + y)

    def at_y(step):
        return (region, x * ny + lax.rem(y + step, ny))

    def at_z(step):
        return (lax.rem(z + step, nz) * 2 + core, pos)

    partners = [(up, left), (down, right), (up, pos), (down, pos), (region, left), (region, right), sibling]
    partners += [at_z(s) for s in range(1, nz)] + [at_y(s) for s in range(1, ny)] + [at_x(s) for s in range(1, nx)]
    barrier = pltpu.get_barrier_semaphore()
    for partner in partners:
        pl.semaphore_signal(barrier, inc=1, device_id=partner, device_id_type=MESH)

    loads = [
        pltpu.make_async_copy(tile, window.at[:, 0:edge, 0:edge], load_sem.at[0]),
        pltpu.make_async_copy(tables_h, tables, load_sem.at[1]),
        pltpu.make_async_copy(probe_h, probe, load_sem.at[2]),
        pltpu.make_async_copy(amp_h, amp, load_sem.at[3]),
    ]
    for load in loads:
        load.start()
    pl.semaphore_wait(barrier, len(partners))

    def send(src, dst, send_sem, recv_sem, device):
        copy = pltpu.make_async_remote_copy(
            src_ref=src, dst_ref=dst, send_sem=send_sem, recv_sem=recv_sem, device_id=device, device_id_type=MESH
        )
        copy.start()
        return copy

    second = slice(edge, 2 * edge)
    first = slice(0, edge)
    halo = [
        send(tile, window.at[:, second, second], halo_send.at[0], halo_recv.at[0], (up, left)),
        send(tile, window.at[:, second, first], halo_send.at[1], halo_recv.at[1], (up, pos)),
        send(tile, window.at[:, first, second], halo_send.at[2], halo_recv.at[2], (region, left)),
    ]
    for load in loads:
        load.wait()
    for copy in halo:
        copy.wait()

    row_limit = jnp.where(region < n_region - 1, 2 * edge, edge)
    col_limit = jnp.where(pos < n_pos - 1, 2 * edge, edge)
    live = counts[0, 0]

    def forward(slot, carry):
        row0, col0 = offsets[0, 0, slot], offsets[0, 1, slot]
        rows = one_hot((edge, 2 * edge), 1, row0, row_limit)
        cols = one_hot((2 * edge, edge), 0, col0, col_limit)
        lines = dot(rows, jnp.concatenate([window[0], window[1]], axis=1)).astype(BF16)
        crop = dot(jnp.concatenate([lines[:, : 2 * edge], lines[:, 2 * edge :]], axis=0), cols)
        crop_r, crop_i = crop[:edge], crop[edge:]
        crops[slot, 0], crops[slot, 1] = crop_r, crop_i
        exits = []
        for m in range(modes):
            probe_r, probe_i = probe[0, m], probe[1, m]
            exits.append(
                jnp.concatenate([probe_r * crop_r - probe_i * crop_i, probe_r * crop_i + probe_i * crop_r], axis=1)
            )
        half = on_right(split(jnp.concatenate(exits, axis=0)), tables.at[0])
        turned = jnp.concatenate(
            [
                jnp.concatenate([half[m * edge : (m + 1) * edge, :edge], half[m * edge : (m + 1) * edge, edge:]], axis=0)
                for m in range(modes)
            ],
            axis=1,
        )
        far = on_left(tables.at[1], split(turned))
        intensity = jnp.zeros((edge, edge), F32)
        for m in range(modes):
            part = far[:, m * edge : (m + 1) * edge]
            intensity += part[:edge] * part[:edge] + part[edge:] * part[edge:]
        factor = 1.0 - amp[0, slot] / jnp.sqrt(intensity + 1.0)
        factor = jnp.where(slot < live, factor, 0.0)
        for m in range(modes):
            lanes = slice(m * edge, (m + 1) * edge)
            high, low = split(far[:, lanes] * jnp.concatenate([factor, factor], axis=0))
            res_high[slot, :, lanes] = high
            res_low[slot, :, lanes] = low
        return carry

    lax.fori_loop(0, slots, forward, 0)

    per = modes // CHUNKS

    def backward_of(chunk):
        def backward(slot, carry):
            lanes = slice(chunk * per * edge, (chunk + 1) * per * edge)
            half = on_left(tables.at[0], (res_high[slot, :, lanes], res_low[slot, :, lanes]))
            turned = jnp.concatenate(
                [
                    jnp.concatenate(
                        [half[:edge, m * edge : (m + 1) * edge], half[edge:, m * edge : (m + 1) * edge]], axis=1
                    )
                    for m in range(per)
                ],
                axis=0,
            )
            back = on_right(split(turned), tables.at[1])
            crop_r, crop_i = crops[slot, 0], crops[slot, 1]
            obj_r, obj_i = 0.0, 0.0
            for m in range(per):
                back_r, back_i = back[m * edge : (m + 1) * edge, :edge], back[m * edge : (m + 1) * edge, edge:]
                probe_r, probe_i = probe[0, chunk * per + m], probe[1, chunk * per + m]
                obj_r += probe_r * back_r + probe_i * back_i
                obj_i += probe_r * back_i - probe_i * back_r
                lines = slice(m * edge, (m + 1) * edge)
                terms[0, chunk, lines] += crop_r * back_r + crop_i * back_i
                terms[1, chunk, lines] += crop_r * back_i - crop_i * back_r
            if chunk == 0:
                obj_terms[slot, 0], obj_terms[slot, 1] = obj_r, obj_i
            else:
                obj_terms[slot, 0] += obj_r
                obj_terms[slot, 1] += obj_i
            return carry

        terms[:, chunk] = jnp.zeros((2, per * edge, edge), F32)
        lax.fori_loop(0, slots, backward, 0)

    def place(slot, carry):
        row0, col0 = offsets[0, 0, slot], offsets[0, 1, slot]
        cols = one_hot((edge, 2 * edge), 1, col0)
        rows = one_hot((2 * edge, edge), 0, row0)
        high_r, low_r = split(obj_terms[slot, 0])
        high_i, low_i = split(obj_terms[slot, 1])
        wide = dot(jnp.concatenate([high_r, high_i, low_r, low_i], axis=0), cols)
        wide = wide[: 2 * edge] + wide[2 * edge :]
        high, low = split(jnp.concatenate([wide[:edge], wide[edge:]], axis=1))
        field = dot(jnp.concatenate([rows, rows], axis=1), jnp.concatenate([high, low], axis=0))
        grads[0] += field[:, : 2 * edge]
        grads[1] += field[:, 2 * edge :]
        return carry

    pending = []
    chunk_rows = per * edge
    x_rows, y_rows = chunk_rows // nx, chunk_rows // nx // ny

    def core_scatter(q):
        copy = send(terms.at[1 - core, q], from_core.at[q], core_send.at[q], core_recv.at[q], sibling)
        pending.append(copy)
        return [copy]

    def x_scatter(q, arrived):
        for copy in arrived:
            copy.wait_recv()
        own[q] = terms[core, q] + from_core[q]
        copies = []
        for s in sorted(range(1, nx), key=lambda s: -min(s, nx - s)):
            rows = pl.ds(pl.multiple_of(lax.rem(x + s, nx) * x_rows, x_rows), x_rows)
            copies.append(
                send(own.at[q, rows], from_x.at[q, s - 1], x_send.at[q, s - 1], x_recv.at[q, s - 1], at_x(s))
            )
        pending.extend(copies)
        return copies

    def y_scatter(q, arrived):
        for copy in arrived:
            copy.wait_recv()
        total = own[q, pl.ds(pl.multiple_of(x * x_rows, x_rows), x_rows)]
        for s in range(1, nx):
            total += from_x[q, s - 1]
        by_x[q] = total
        copies = []
        for s in sorted(range(1, ny), key=lambda s: -min(s, ny - s)):
            rows = pl.ds(pl.multiple_of(lax.rem(y + s, ny) * y_rows, y_rows), y_rows)
            copies.append(
                send(by_x.at[q, rows], from_y.at[q, s - 1], y_send.at[q, s - 1], y_recv.at[q, s - 1], at_y(s))
            )
        pending.extend(copies)
        return copies

    def z_gather(q, arrived):
        for copy in arrived:
            copy.wait_recv()
        total = by_x[q, pl.ds(pl.multiple_of(y * y_rows, y_rows), y_rows)]
        for s in range(1, ny):
            total += from_y[q, s - 1]
        by_z[q, z] = total
        copies = []
        for s in sorted(range(1, nz), key=lambda s: -min(s, nz - s)):
            copies.append(
                send(by_z.at[q, z], by_z.at[q, z], z_send.at[q, s - 1], z_recv.at[q, s - 1], at_z(s))
            )
        pending.extend(copies)
        return copies

    def y_gather(q, arrived):
        for copy in arrived:
            copy.wait_recv()
        total = by_z[q, 0]
        for s in range(1, nz):
            total += by_z[q, s]
        mine = probe_out.at[core, q, pl.ds(pl.multiple_of(x * x_rows + y * y_rows, y_rows), y_rows)]
        mine[...] = total * scale
        copies = []
        for s in sorted(range(1, ny), key=lambda s: -min(s, ny - s)):
            copies.append(send(mine, mine, gy_send.at[q, s - 1], gy_recv.at[q, s - 1], at_y(s)))
        pending.extend(copies)
        return copies

    def x_gather(q, arrived):
        for copy in arrived:
            copy.wait_recv()
        mine = probe_out.at[core, q, pl.ds(pl.multiple_of(x * x_rows, x_rows), x_rows)]
        copies = []
        for s in sorted(range(1, nx), key=lambda s: -min(s, nx - s)):
            copies.append(send(mine, mine, gx_send.at[q, s - 1], gx_recv.at[q, s - 1], at_x(s)))
        pending.extend(copies)
        return copies

    def core_gather(q, arrived):
        for copy in arrived:
            copy.wait_recv()
        mine = probe_out.at[core, q]
        copy = send(mine, mine, gc_send.at[q], gc_recv.at[q], sibling)
        pending.append(copy)
        return [copy]

    backward_of(0)
    state = [core_scatter(0), None]
    backward_of(1)
    state[1] = core_scatter(1)
    state[0] = x_scatter(0, state[0])
    grads[...] = jnp.zeros_like(grads)
    lax.fori_loop(0, slots, place, 0)
    state[1] = x_scatter(1, state[1])
    state[0] = y_scatter(0, state[0])
    grad_copies = [
        send(grads.at[:, second, second], from_grad.at[0], grad_send.at[0], grad_recv.at[0], (down, right)),
        send(grads.at[:, second, first], from_grad.at[1], grad_send.at[1], grad_recv.at[1], (down, pos)),
        send(grads.at[:, first, second], from_grad.at[2], grad_send.at[2], grad_recv.at[2], (region, right)),
    ]
    for phase in (y_scatter, z_gather, y_gather, x_gather, core_gather):
        if phase is not y_scatter:
            state[0] = phase(0, state[0])
        state[1] = phase(1, state[1])
        if phase is z_gather:
            for copy in grad_copies:
                copy.wait()
            total = grads[:, first, first]
            total += jnp.where(pos > 0, from_grad[2], 0.0)
            total += jnp.where(region > 0, from_grad[1], 0.0)
            total += jnp.where(jnp.logical_and(region > 0, pos > 0), from_grad[0], 0.0)
            obj_out[...] = total
    for copies in state:
        for copy in copies:
            copy.wait_recv()
    for copy in pending:
        copy.wait_send()


def solution(mesh):
    n_region, n_pos = mesh.shape["region"], mesh.shape["pos"]
    nz = n_region // 2
    nx = 4 if n_pos == 32 else 2
    ny = n_pos // nx

    def on_device(object_tiles, probe, amplitudes, offsets, counts):
        modes, edge = probe.shape[1], probe.shape[2]
        slots = amplitudes.shape[1]
        rows = modes // CHUNKS * edge
        x_rows, y_rows = rows // nx, rows // nx // ny
        scale = 1.0 / math.sqrt(n_region * n_pos * slots)
        dma = pltpu.SemaphoreType.DMA
        any_space = pl.BlockSpec(memory_space=pl.ANY)
        vmem_space = pl.BlockSpec(memory_space=pltpu.VMEM)
        smem_space = pl.BlockSpec(memory_space=pltpu.SMEM)
        sizes = (nx, ny, nz, slots, modes, edge)
        phase_sems = []
        for count in (0, nx - 1, ny - 1, nz - 1, ny - 1, nx - 1, 0):
            shape = (CHUNKS, count) if count else (CHUNKS,)
            phase_sems += [dma(shape), dma(shape)]
        obj_grad, probe_grad = pl.pallas_call(
            functools.partial(kernel, sizes, scale),
            out_shape=(
                jax.ShapeDtypeStruct((2, edge, edge), F32),
                jax.ShapeDtypeStruct((2, CHUNKS, rows, edge), F32),
            ),
            in_specs=[vmem_space, any_space, any_space, smem_space, smem_space, any_space],
            out_specs=(vmem_space, vmem_space),
            scratch_shapes=[
                pltpu.VMEM((2, 2 * edge, 2 * edge), BF16),
                pltpu.VMEM((2, modes, edge, edge), F32),
                pltpu.VMEM((1, slots, edge, edge), F32),
                pltpu.VMEM((2, 2, 2 * edge, 2 * edge), BF16),
                pltpu.VMEM((slots, 2, edge, edge), F32),
                pltpu.VMEM((slots, 2 * edge, modes * edge), BF16),
                pltpu.VMEM((slots, 2 * edge, modes * edge), BF16),
                pltpu.VMEM((slots, 2, edge, edge), F32),
                pltpu.VMEM((2, 2 * edge, 2 * edge), F32),
                pltpu.VMEM((2, CHUNKS, rows, edge), F32),
                pltpu.VMEM((CHUNKS, rows, edge), F32),
                pltpu.VMEM((CHUNKS, rows, edge), F32),
                pltpu.VMEM((CHUNKS, x_rows, edge), F32),
                pltpu.VMEM((CHUNKS, nx - 1, x_rows, edge), F32),
                pltpu.VMEM((CHUNKS, y_rows, edge), F32),
                pltpu.VMEM((CHUNKS, ny - 1, y_rows, edge), F32),
                pltpu.VMEM((CHUNKS, nz, y_rows, edge), F32),
                pltpu.VMEM((3, 2, edge, edge), F32),
                dma((4,)), dma((3,)), dma((3,)), dma((3,)), dma((3,)),
                *phase_sems,
            ],
            compiler_params=pltpu.CompilerParams(collective_id=0, has_side_effects=True),
        )(object_tiles, probe, amplitudes, offsets, counts, jnp.asarray(dft_parts(edge)))
        return obj_grad, probe_grad.reshape(2, modes, edge, edge)

    return jax.shard_map(
        on_device,
        mesh=mesh,
        in_specs=(
            P(None, "region", "pos"),
            P(),
            P("region", "pos", None, None),
            P("region", None, "pos"),
            P("region", "pos"),
        ),
        out_specs=(P(None, "region", "pos"), P()),
        check_vma=False,
    )
```

```python
import functools
import math

import jax
import jax.numpy as jnp
import numpy as np
from jax import lax
from jax.experimental import pallas as pl
from jax.experimental.pallas import tpu as pltpu
from jax.sharding import PartitionSpec as P

MESH = pl.DeviceIdType.MESH
F32 = jnp.float32
BF16 = jnp.bfloat16
CHUNKS = 2
GROUP = 2
UNROLL = 1


def dft_parts(order):
    index = np.arange(order)
    angle = (index[:, None] * index[None, :] % order) * (2.0 * math.pi / order)
    cos, sin = np.cos(angle) / math.sqrt(order), np.sin(angle) / math.sqrt(order)
    right = np.block([[cos, -sin], [sin, cos]]).astype(np.float32)
    parts = []
    for table in (right, right.T):
        high = table.astype(jnp.bfloat16)
        low = (table - high.astype(np.float32)).astype(jnp.bfloat16)
        parts.append(np.stack([high, low]))
    return np.stack(parts)


def split(value):
    high = value.astype(BF16)
    return high, (value - high.astype(F32)).astype(BF16)


def dot(a, b):
    return jnp.dot(a, b, preferred_element_type=F32)


def on_left(table, value):
    high, low = value
    return dot(
        jnp.concatenate([table[0], table[0], table[1]], axis=1),
        jnp.concatenate([high, low, high], axis=0),
    )


def on_right(value, table):
    high, low = value
    return dot(
        jnp.concatenate([high, low, high], axis=1),
        jnp.concatenate([table[0], table[0], table[1]], axis=0),
    )


def one_hot(shape, dim, shift, limit=None):
    along = lax.broadcasted_iota(jnp.int32, shape, dim)
    other = lax.broadcasted_iota(jnp.int32, shape, 1 - dim)
    hit = along == other + shift
    if limit is not None:
        hit = jnp.logical_and(hit, along < limit)
    return jnp.where(hit, 1.0, 0.0).astype(BF16)


def by_distance(count):
    return sorted(range(1, count), key=lambda step: -min(step, count - step))


def kernel(
    sizes, scale, tile, probe_h, amp_h, offsets_h, counts_h, tables_h, obj_out, probe_out,
    offsets, counts, window, probe, amp, tables, crops, res_high, res_low, backs, grads, terms, own, from_core, by_x,
    from_x, from_y, by_z, from_grad, load_sem, halo_send, halo_recv, grad_send, grad_recv, core_send, core_recv,
    x_send, x_recv, y_send, y_recv, z_send, z_recv, gy_send, gy_recv, gx_send, gx_recv, gc_send, gc_recv,
):
    nx, ny, nz, slots, modes, edge = sizes
    region, pos = lax.axis_index("region"), lax.axis_index("pos")
    n_region, n_pos = 2 * nz, nx * ny
    z, core = region // 2, lax.rem(region, 2)
    x, y = pos // ny, lax.rem(pos, ny)
    up, down = lax.rem(region + n_region - 1, n_region), lax.rem(region + 1, n_region)
    left, right = lax.rem(pos + n_pos - 1, n_pos), lax.rem(pos + 1, n_pos)
    sibling = (region + 1 - 2 * core, pos)

    def at_x(step):
        return (region, lax.rem(x + step, nx) * ny + y)

    def at_y(step):
        return (region, x * ny + lax.rem(y + step, ny))

    def at_z(step):
        return (lax.rem(z + step, nz) * 2 + core, pos)

    partners = [(down, right), (down, pos), (region, right), (up, left), (up, pos), (region, left), sibling]
    partners += [at_z(s) for s in by_distance(nz)] + [at_y(s) for s in by_distance(ny)]
    partners += [at_x(s) for s in by_distance(nx)]
    barrier = pltpu.get_barrier_semaphore()
    for partner in partners:
        pl.semaphore_signal(barrier, inc=1, device_id=partner, device_id_type=MESH)

    first, second = slice(0, edge), slice(edge, 2 * edge)
    loads = [
        pltpu.make_async_copy(offsets_h, offsets, load_sem.at[0]),
        pltpu.make_async_copy(counts_h, counts, load_sem.at[1]),
        pltpu.make_async_copy(tile, window.at[:, first, first], load_sem.at[2]),
        pltpu.make_async_copy(probe_h, probe, load_sem.at[3]),
        pltpu.make_async_copy(tables_h, tables, load_sem.at[4]),
        pltpu.make_async_copy(amp_h, amp, load_sem.at[5]),
    ]
    for load in loads:
        load.start()
    pl.semaphore_wait(barrier, len(partners))

    def send(src, dst, send_sem, recv_sem, device):
        copy = pltpu.make_async_remote_copy(
            src_ref=src, dst_ref=dst, send_sem=send_sem, recv_sem=recv_sem, device_id=device, device_id_type=MESH
        )
        copy.start()
        return copy

    halo = [
        send(tile, window.at[:, second, second], halo_send.at[0], halo_recv.at[0], (up, left)),
        send(tile, window.at[:, first, second], halo_send.at[2], halo_recv.at[2], (region, left)),
        send(tile, window.at[:, second, first], halo_send.at[1], halo_recv.at[1], (up, pos)),
    ]
    for load in loads:
        load.wait()
    for copy in halo:
        copy.wait()

    row_limit = jnp.where(region < n_region - 1, 2 * edge, edge)
    col_limit = jnp.where(pos < n_pos - 1, 2 * edge, edge)
    live = counts[0, 0]

    def forward(slot, carry):
        row0, col0 = offsets[0, 0, slot], offsets[0, 1, slot]
        rows = one_hot((edge, 2 * edge), 1, row0, row_limit)
        cols = one_hot((2 * edge, edge), 0, col0, col_limit)
        lines = dot(rows, jnp.concatenate([window[0], window[1]], axis=1)).astype(BF16)
        crop = dot(jnp.concatenate([lines[:, : 2 * edge], lines[:, 2 * edge :]], axis=0), cols)
        crop_r, crop_i = crop[:edge], crop[edge:]
        crops[slot, 0], crops[slot, 1] = crop_r, crop_i
        intensity = jnp.zeros((edge, edge), F32)
        fars = []
        for m in range(0, modes, GROUP):
            exits = []
            for n in range(m, m + GROUP):
                probe_r, probe_i = probe[0, n], probe[1, n]
                exits.append(
                    jnp.concatenate([probe_r * crop_r - probe_i * crop_i, probe_r * crop_i + probe_i * crop_r], axis=1)
                )
            half = on_right(split(jnp.concatenate(exits, axis=0)), tables.at[0])
            blocks = [half[n * edge : (n + 1) * edge] for n in range(GROUP)]
            turned = jnp.concatenate(
                [jnp.concatenate([block[:, :edge], block[:, edge:]], axis=0) for block in blocks], axis=1
            )
            far = on_left(tables.at[1], split(turned))
            for n in range(GROUP):
                part = far[:, n * edge : (n + 1) * edge]
                intensity += part[:edge] * part[:edge] + part[edge:] * part[edge:]
                fars.append(part)
        factor = 1.0 - amp[0, slot] / jnp.sqrt(intensity + 1.0)
        factor = jnp.where(slot < live, factor, 0.0)
        factor = jnp.concatenate([factor, factor], axis=0)
        for m in range(modes):
            high, low = split(fars[m] * factor)
            res_high[slot, m], res_low[slot, m] = high, low
        return carry

    lax.fori_loop(0, slots, forward, 0, unroll=UNROLL)

    per = modes // CHUNKS

    def backward_of(chunk):
        def backward(slot, carry):
            picks = range(chunk * per, (chunk + 1) * per)
            high = jnp.concatenate([res_high[slot, m] for m in picks], axis=1)
            low = jnp.concatenate([res_low[slot, m] for m in picks], axis=1)
            half = on_left(tables.at[0], (high, low))
            blocks = [half[:, n * edge : (n + 1) * edge] for n in range(per)]
            turned = jnp.concatenate(
                [jnp.concatenate([block[:edge], block[edge:]], axis=1) for block in blocks], axis=0
            )
            back = on_right(split(turned), tables.at[1])
            backs[slot, chunk] = back
            crop_r, crop_i = crops[slot, 0], crops[slot, 1]
            for n in range(per):
                lines = slice(n * edge, (n + 1) * edge)
                back_r, back_i = back[lines, :edge], back[lines, edge:]
                term_r = crop_r * back_r + crop_i * back_i
                term_i = crop_r * back_i - crop_i * back_r
                terms[0, chunk, lines] += term_r
                terms[1, chunk, lines] += term_i
            return carry

        return backward

    def place(slot):
        row0, col0 = offsets[0, 0, slot], offsets[0, 1, slot]
        cols = one_hot((edge, 2 * edge), 1, col0)
        rows = one_hot((2 * edge, edge), 0, row0)
        obj_r, obj_i = 0.0, 0.0
        for m in range(modes):
            lines = slice(m % per * edge, (m % per + 1) * edge)
            back_r, back_i = backs[slot, m // per, lines, first], backs[slot, m // per, lines, second]
            probe_r, probe_i = probe[0, m], probe[1, m]
            obj_r += probe_r * back_r + probe_i * back_i
            obj_i += probe_r * back_i - probe_i * back_r
        high_r, low_r = split(obj_r)
        high_i, low_i = split(obj_i)
        wide = dot(jnp.concatenate([high_r, high_i, low_r, low_i], axis=0), cols)
        wide = wide[: 2 * edge] + wide[2 * edge :]
        high, low = split(jnp.concatenate([wide[:edge], wide[edge:]], axis=1))
        field = dot(jnp.concatenate([rows, rows], axis=1), jnp.concatenate([high, low], axis=0))
        if slot == 0:
            grads[0], grads[1] = field[:, : 2 * edge], field[:, 2 * edge :]
        else:
            grads[0] += field[:, : 2 * edge]
            grads[1] += field[:, 2 * edge :]

    pending = []
    chunk_rows = per * edge
    x_rows, y_rows = chunk_rows // nx, chunk_rows // nx // ny

    def x_lines(step=0):
        return pl.ds(pl.multiple_of(lax.rem(x + step, nx) * x_rows, x_rows), x_rows)

    def y_lines(step=0):
        return pl.ds(pl.multiple_of(lax.rem(y + step, ny) * y_rows, y_rows), y_rows)

    def sent(copies):
        pending.extend(copies)
        return copies

    def core_scatter(q):
        return sent([send(terms.at[1 - core, q], from_core.at[q], core_send.at[q], core_recv.at[q], sibling)])

    def x_scatter(q, arrived):
        for copy in arrived:
            copy.wait_recv()
        own[q] = terms[core, q] + from_core[q]
        return sent(
            [
                send(own.at[q, x_lines(s)], from_x.at[q, s - 1], x_send.at[q, s - 1], x_recv.at[q, s - 1], at_x(s))
                for s in by_distance(nx)
            ]
        )

    def y_scatter(q, arrived):
        for copy in arrived:
            copy.wait_recv()
        total = own[q, x_lines()]
        for s in range(1, nx):
            total += from_x[q, s - 1]
        by_x[q] = total
        return sent(
            [
                send(by_x.at[q, y_lines(s)], from_y.at[q, s - 1], y_send.at[q, s - 1], y_recv.at[q, s - 1], at_y(s))
                for s in by_distance(ny)
            ]
        )

    def z_gather(q, arrived):
        for copy in arrived:
            copy.wait_recv()
        total = by_x[q, y_lines()]
        for s in range(1, ny):
            total += from_y[q, s - 1]
        by_z[q, z] = total
        return sent(
            [
                send(by_z.at[q, z], by_z.at[q, z], z_send.at[q, s - 1], z_recv.at[q, s - 1], at_z(s))
                for s in by_distance(nz)
            ]
        )

    def y_gather(q, arrived):
        for copy in arrived:
            copy.wait_recv()
        total = by_z[q, 0]
        for s in range(1, nz):
            total += by_z[q, s]
        mine = probe_out.at[core, q, pl.ds(pl.multiple_of(x * x_rows + y * y_rows, y_rows), y_rows)]
        mine[...] = total * scale
        return sent(
            [send(mine, mine, gy_send.at[q, s - 1], gy_recv.at[q, s - 1], at_y(s)) for s in by_distance(ny)]
        )

    def x_gather(q, arrived):
        for copy in arrived:
            copy.wait_recv()
        mine = probe_out.at[core, q, x_lines()]
        copies = sent([send(mine, mine, gx_send.at[q, s - 1], gx_recv.at[q, s - 1], at_x(s)) for s in by_distance(nx)])
        to_core = sent([send(mine, mine, gc_send.at[q, 0], gc_recv.at[q, 0], sibling)])
        return copies, to_core

    def core_gather(q, arrived):
        copies, to_core = arrived
        steps = by_distance(nx)
        for s, copy in sorted(zip(steps, copies), key=lambda pair: min(pair[0], nx - pair[0])):
            copy.wait_recv()
            piece = probe_out.at[core, q, x_lines(nx - s)]
            to_core += sent([send(piece, piece, gc_send.at[q, s], gc_recv.at[q, s], sibling)])
        return to_core

    terms[...] = jnp.zeros_like(terms)
    lax.fori_loop(0, slots, backward_of(0), 0, unroll=UNROLL)
    front = core_scatter(0)
    lax.fori_loop(0, slots // 2, backward_of(1), 0, unroll=UNROLL)
    front = x_scatter(0, front)
    lax.fori_loop(slots // 2, slots, backward_of(1), 0, unroll=UNROLL)
    back = core_scatter(1)
    place(0)
    back = x_scatter(1, back)
    front = y_scatter(0, front)
    for slot in range(1, max(2, slots // 2)):
        place(slot)
    back = y_scatter(1, back)
    front = z_gather(0, front)
    for slot in range(max(2, slots // 2), slots):
        place(slot)
    grad_copies = [
        send(grads.at[:, second, second], from_grad.at[0], grad_send.at[0], grad_recv.at[0], (down, right)),
        send(grads.at[:, first, second], from_grad.at[2], grad_send.at[2], grad_recv.at[2], (region, right)),
        send(grads.at[:, second, first], from_grad.at[1], grad_send.at[1], grad_recv.at[1], (down, pos)),
    ]
    back = z_gather(1, back)
    front = y_gather(0, front)
    back = y_gather(1, back)
    front = x_gather(0, front)
    for copy in grad_copies:
        copy.wait()
    total = grads[:, first, first]
    total += jnp.where(pos > 0, from_grad[2], 0.0)
    total += jnp.where(region > 0, from_grad[1], 0.0)
    total += jnp.where(jnp.logical_and(region > 0, pos > 0), from_grad[0], 0.0)
    obj_out[...] = total
    back = x_gather(1, back)
    front = core_gather(0, front)
    back = core_gather(1, back)
    for copy in front + back:
        copy.wait_recv()
    for copy in pending:
        copy.wait_send()


def finish(obj_in, probe_in, obj_out, probe_out, sems):
    copies = [
        pltpu.make_async_copy(probe_in, probe_out, sems.at[0]),
        pltpu.make_async_copy(obj_in, obj_out, sems.at[1]),
    ]
    for copy in copies:
        copy.start()
    for copy in copies:
        copy.wait()


def solution(mesh):
    n_region, n_pos = mesh.shape["region"], mesh.shape["pos"]
    nz = n_region // 2
    nx = 4 if n_pos == 32 else 2
    ny = n_pos // nx

    def on_device(object_tiles, probe, amplitudes, offsets, counts):
        modes, edge = probe.shape[1], probe.shape[2]
        slots = amplitudes.shape[1]
        rows = modes // CHUNKS * edge
        x_rows, y_rows = rows // nx, rows // nx // ny
        scale = 1.0 / math.sqrt(n_region * n_pos * slots)
        dma = pltpu.SemaphoreType.DMA
        any_space = pl.BlockSpec(memory_space=pl.ANY)
        vmem_space = pl.BlockSpec(memory_space=pltpu.VMEM)
        sizes = (nx, ny, nz, slots, modes, edge)
        phase_sems = []
        for count in (0, nx - 1, ny - 1, nz - 1, ny - 1, nx - 1, nx):
            shape = (CHUNKS, count) if count else (CHUNKS,)
            phase_sems += [dma(shape), dma(shape)]
        held = pl.pallas_call(
            functools.partial(kernel, sizes, scale),
            out_shape=(pltpu.VMEM((2, edge, edge), F32), pltpu.VMEM((2, CHUNKS, rows, edge), F32)),
            in_specs=[any_space] * 6,
            out_specs=(vmem_space, vmem_space),
            scratch_shapes=[
                pltpu.SMEM((1, 2, slots), jnp.int32),
                pltpu.SMEM((1, 1), jnp.int32),
                pltpu.VMEM((2, 2 * edge, 2 * edge), BF16),
                pltpu.VMEM((2, modes, edge, edge), F32),
                pltpu.VMEM((1, slots, edge, edge), F32),
                pltpu.VMEM((2, 2, 2 * edge, 2 * edge), BF16),
                pltpu.VMEM((slots, 2, edge, edge), F32),
                pltpu.VMEM((slots, modes, 2 * edge, edge), BF16),
                pltpu.VMEM((slots, modes, 2 * edge, edge), BF16),
                pltpu.VMEM((slots, CHUNKS, rows, 2 * edge), F32),
                pltpu.VMEM((2, 2 * edge, 2 * edge), F32),
                pltpu.VMEM((2, CHUNKS, rows, edge), F32),
                pltpu.VMEM((CHUNKS, rows, edge), F32),
                pltpu.VMEM((CHUNKS, rows, edge), F32),
                pltpu.VMEM((CHUNKS, x_rows, edge), F32),
                pltpu.VMEM((CHUNKS, nx - 1, x_rows, edge), F32),
                pltpu.VMEM((CHUNKS, ny - 1, y_rows, edge), F32),
                pltpu.VMEM((CHUNKS, nz, y_rows, edge), F32),
                pltpu.VMEM((3, 2, edge, edge), F32),
                dma((6,)), dma((3,)), dma((3,)), dma((3,)), dma((3,)),
                *phase_sems,
            ],
            compiler_params=pltpu.CompilerParams(collective_id=0, has_side_effects=True),
        )(object_tiles, probe, amplitudes, offsets, counts, jnp.asarray(dft_parts(edge)))
        obj_grad, probe_grad = pl.pallas_call(
            finish,
            out_shape=(
                jax.ShapeDtypeStruct((2, edge, edge), F32),
                jax.ShapeDtypeStruct((2, CHUNKS, rows, edge), F32),
            ),
            in_specs=[vmem_space] * 2,
            out_specs=(any_space, any_space),
            scratch_shapes=[dma((2,))],
        )(*[pltpu.with_memory_space_constraint(v, pltpu.VMEM) for v in held])
        return obj_grad, probe_grad.reshape(2, modes, edge, edge)

    return jax.shard_map(
        on_device,
        mesh=mesh,
        in_specs=(
            P(None, "region", "pos"),
            P(),
            P("region", "pos", None, None),
            P("region", None, "pos"),
            P("region", "pos"),
        ),
        out_specs=(P(None, "region", "pos"), P()),
        check_vma=False,
    )
```

```python
import functools
import math

import jax
import jax.numpy as jnp
import numpy as np
from jax import lax
from jax.experimental import pallas as pl
from jax.experimental.pallas import tpu as pltpu
from jax.sharding import PartitionSpec as P

MESH = pl.DeviceIdType.MESH
F32 = jnp.float32
BF16 = jnp.bfloat16
CHUNKS = 2
GROUP = 2


def dft_parts(order):
    index = np.arange(order)
    angle = (index[:, None] * index[None, :] % order) * (2.0 * math.pi / order)
    cos, sin = np.cos(angle) / math.sqrt(order), np.sin(angle) / math.sqrt(order)
    right = np.block([[cos, -sin], [sin, cos]]).astype(np.float32)
    parts = []
    for table in (right, right.T):
        high = table.astype(jnp.bfloat16)
        low = (table - high.astype(np.float32)).astype(jnp.bfloat16)
        parts.append(np.stack([high, low]))
    return np.stack(parts)


def split(value):
    high = value.astype(BF16)
    return high, (value - high.astype(F32)).astype(BF16)


def dot(a, b):
    return jnp.dot(a, b, preferred_element_type=F32)


def on_left(table, value):
    high, low = value
    return dot(
        jnp.concatenate([table[0], table[0], table[1]], axis=1),
        jnp.concatenate([high, low, high], axis=0),
    )


def on_right(value, table):
    high, low = value
    return dot(
        jnp.concatenate([high, low, high], axis=1),
        jnp.concatenate([table[0], table[0], table[1]], axis=0),
    )


def one_hot(shape, dim, shift, limit=None):
    along = lax.broadcasted_iota(jnp.int32, shape, dim)
    other = lax.broadcasted_iota(jnp.int32, shape, 1 - dim)
    hit = along == other + shift
    if limit is not None:
        hit = jnp.logical_and(hit, along < limit)
    return jnp.where(hit, 1.0, 0.0).astype(BF16)


def by_distance(count):
    return sorted(range(1, count), key=lambda step: -min(step, count - step))


def kernel(
    sizes, scale, tile, probe_h, amp_h, offsets_h, counts_h, tables_h, obj_out, probe_out,
    offsets, counts, window, probe, amp, tables, crops, res_high, res_low, backs, grads, terms, own, from_core, by_x,
    from_x, from_y, by_z, from_grad, load_sem, halo_send, halo_recv, grad_send, grad_recv, core_send, core_recv,
    x_send, x_recv, y_send, y_recv, z_send, z_recv, gy_send, gy_recv, gx_send, gx_recv, gc_send, gc_recv,
):
    nx, ny, nz, slots, modes, edge = sizes
    region, pos = lax.axis_index("region"), lax.axis_index("pos")
    n_region, n_pos = 2 * nz, nx * ny
    z, core = region // 2, lax.rem(region, 2)
    x, y = pos // ny, lax.rem(pos, ny)
    up, down = lax.rem(region + n_region - 1, n_region), lax.rem(region + 1, n_region)
    left, right = lax.rem(pos + n_pos - 1, n_pos), lax.rem(pos + 1, n_pos)
    sibling = (region + 1 - 2 * core, pos)

    def at_x(step):
        return (region, lax.rem(x + step, nx) * ny + y)

    def at_y(step):
        return (region, x * ny + lax.rem(y + step, ny))

    def at_z(step):
        return (lax.rem(z + step, nz) * 2 + core, pos)

    partners = [(down, right), (down, pos), (region, right), (up, left), (up, pos), (region, left), sibling]
    partners += [at_z(s) for s in by_distance(nz)] + [at_y(s) for s in by_distance(ny)]
    partners += [at_x(s) for s in by_distance(nx)]
    barrier = pltpu.get_barrier_semaphore()
    for partner in partners:
        pl.semaphore_signal(barrier, inc=1, device_id=partner, device_id_type=MESH)

    first, second = slice(0, edge), slice(edge, 2 * edge)
    loads = [
        pltpu.make_async_copy(offsets_h, offsets, load_sem.at[0]),
        pltpu.make_async_copy(counts_h, counts, load_sem.at[1]),
        pltpu.make_async_copy(tile, window.at[:, first, first], load_sem.at[2]),
        pltpu.make_async_copy(probe_h, probe, load_sem.at[3]),
        pltpu.make_async_copy(tables_h, tables, load_sem.at[4]),
        pltpu.make_async_copy(amp_h, amp, load_sem.at[5]),
    ]
    for load in loads:
        load.start()
    pl.semaphore_wait(barrier, len(partners))

    def send(src, dst, send_sem, recv_sem, device):
        copy = pltpu.make_async_remote_copy(
            src_ref=src, dst_ref=dst, send_sem=send_sem, recv_sem=recv_sem, device_id=device, device_id_type=MESH
        )
        copy.start()
        return copy

    halo = [
        send(tile, window.at[:, second, second], halo_send.at[0], halo_recv.at[0], (up, left)),
        send(tile, window.at[:, first, second], halo_send.at[2], halo_recv.at[2], (region, left)),
        send(tile, window.at[:, second, first], halo_send.at[1], halo_recv.at[1], (up, pos)),
    ]
    for load in loads:
        load.wait()
    for copy in halo:
        copy.wait()

    row_limit = jnp.where(region < n_region - 1, 2 * edge, edge)
    col_limit = jnp.where(pos < n_pos - 1, 2 * edge, edge)
    live = counts[0, 0]

    def crop_at(slot):
        row0, col0 = offsets[0, 0, slot], offsets[0, 1, slot]
        rows = one_hot((edge, 2 * edge), 1, row0, row_limit)
        cols = one_hot((2 * edge, edge), 0, col0, col_limit)
        lines = dot(rows, jnp.concatenate([window[0], window[1]], axis=1)).astype(BF16)
        crop = dot(jnp.concatenate([lines[:, : 2 * edge], lines[:, 2 * edge :]], axis=0), cols)
        crops[slot, 0], crops[slot, 1] = crop[:edge], crop[edge:]

    def rows_of(slot, m):
        crop_r, crop_i = crops[slot, 0], crops[slot, 1]
        exits = []
        for n in range(m, m + GROUP):
            probe_r, probe_i = probe[0, n], probe[1, n]
            exits.append(
                jnp.concatenate([probe_r * crop_r - probe_i * crop_i, probe_r * crop_i + probe_i * crop_r], axis=1)
            )
        half = on_right(split(jnp.concatenate(exits, axis=0)), tables.at[0])
        for n in range(GROUP):
            block = half[n * edge : (n + 1) * edge]
            high, low = split(jnp.concatenate([block[:, :edge], block[:, edge:]], axis=0))
            res_high[slot, m + n], res_low[slot, m + n] = high, low

    def columns_of(slot, m):
        picks = range(m, m + GROUP)
        high = jnp.concatenate([res_high[slot, n] for n in picks], axis=1)
        low = jnp.concatenate([res_low[slot, n] for n in picks], axis=1)
        far = on_left(tables.at[1], (high, low))
        return [far[:, n * edge : (n + 1) * edge] for n in range(GROUP)]

    def residual(slot, fars):
        intensity = jnp.zeros((edge, edge), F32)
        for part in fars:
            intensity += part[:edge] * part[:edge] + part[edge:] * part[edge:]
        factor = 1.0 - amp[0, slot] / jnp.sqrt(intensity + 1.0)
        factor = jnp.where(slot < live, factor, 0.0)
        factor = jnp.concatenate([factor, factor], axis=0)
        for m in range(modes):
            high, low = split(fars[m] * factor)
            res_high[slot, m], res_low[slot, m] = high, low

    for slot in range(slots):
        crop_at(slot)
    for m in range(0, modes, GROUP):
        rows_of(0, m)
    for slot in range(slots):
        fars = []
        for m in range(0, modes, GROUP):
            if slot + 1 < slots:
                rows_of(slot + 1, m)
            fars += columns_of(slot, m)
        residual(slot, fars)

    per = modes // CHUNKS

    def back_columns(chunk, slot):
        picks = range(chunk * per, (chunk + 1) * per)
        high = jnp.concatenate([res_high[slot, m] for m in picks], axis=1)
        low = jnp.concatenate([res_low[slot, m] for m in picks], axis=1)
        half = on_left(tables.at[0], (high, low))
        for n, m in enumerate(picks):
            res_high[slot, m], res_low[slot, m] = split(half[:, n * edge : (n + 1) * edge])

    def back_rows(chunk, slot):
        parts = []
        for ref in (res_high, res_low):
            blocks = [ref[slot, m] for m in range(chunk * per, (chunk + 1) * per)]
            parts.append(
                jnp.concatenate([jnp.concatenate([block[:edge], block[edge:]], axis=1) for block in blocks], axis=0)
            )
        back = on_right(parts, tables.at[1])
        backs[slot, chunk] = back
        crop_r, crop_i = crops[slot, 0], crops[slot, 1]
        for n in range(per):
            lines = slice(n * edge, (n + 1) * edge)
            back_r, back_i = back[lines, :edge], back[lines, edge:]
            term_r = crop_r * back_r + crop_i * back_i
            term_i = crop_r * back_i - crop_i * back_r
            if slot == 0:
                terms[0, chunk, lines], terms[1, chunk, lines] = term_r, term_i
            else:
                terms[0, chunk, lines] += term_r
                terms[1, chunk, lines] += term_i

    def place(slot):
        row0, col0 = offsets[0, 0, slot], offsets[0, 1, slot]
        cols = one_hot((edge, 2 * edge), 1, col0)
        rows = one_hot((2 * edge, edge), 0, row0)
        obj_r, obj_i = 0.0, 0.0
        for m in range(modes):
            lines = slice(m % per * edge, (m % per + 1) * edge)
            back_r, back_i = backs[slot, m // per, lines, first], backs[slot, m // per, lines, second]
            probe_r, probe_i = probe[0, m], probe[1, m]
            obj_r += probe_r * back_r + probe_i * back_i
            obj_i += probe_r * back_i - probe_i * back_r
        high_r, low_r = split(obj_r)
        high_i, low_i = split(obj_i)
        wide = dot(jnp.concatenate([high_r, high_i, low_r, low_i], axis=0), cols)
        wide = wide[: 2 * edge] + wide[2 * edge :]
        high, low = split(jnp.concatenate([wide[:edge], wide[edge:]], axis=1))
        field = dot(jnp.concatenate([rows, rows], axis=1), jnp.concatenate([high, low], axis=0))
        if slot == 0:
            grads[0], grads[1] = field[:, : 2 * edge], field[:, 2 * edge :]
        else:
            grads[0] += field[:, : 2 * edge]
            grads[1] += field[:, 2 * edge :]

    pending = []
    chunk_rows = per * edge
    x_rows, y_rows = chunk_rows // nx, chunk_rows // nx // ny

    def x_lines(step=0):
        return pl.ds(pl.multiple_of(lax.rem(x + step, nx) * x_rows, x_rows), x_rows)

    def y_lines(step=0):
        return pl.ds(pl.multiple_of(lax.rem(y + step, ny) * y_rows, y_rows), y_rows)

    def sent(copies):
        pending.extend(copies)
        return copies

    def core_scatter(q):
        return sent([send(terms.at[1 - core, q], from_core.at[q], core_send.at[q], core_recv.at[q], sibling)])

    def x_scatter(q, arrived):
        for copy in arrived:
            copy.wait_recv()
        own[q] = terms[core, q] + from_core[q]
        return sent(
            [
                send(own.at[q, x_lines(s)], from_x.at[q, s - 1], x_send.at[q, s - 1], x_recv.at[q, s - 1], at_x(s))
                for s in by_distance(nx)
            ]
        )

    def y_scatter(q, arrived):
        for copy in arrived:
            copy.wait_recv()
        total = own[q, x_lines()]
        for s in range(1, nx):
            total += from_x[q, s - 1]
        by_x[q] = total
        return sent(
            [
                send(by_x.at[q, y_lines(s)], from_y.at[q, s - 1], y_send.at[q, s - 1], y_recv.at[q, s - 1], at_y(s))
                for s in by_distance(ny)
            ]
        )

    def z_gather(q, arrived):
        for copy in arrived:
            copy.wait_recv()
        total = by_x[q, y_lines()]
        for s in range(1, ny):
            total += from_y[q, s - 1]
        by_z[q, z] = total
        return sent(
            [
                send(by_z.at[q, z], by_z.at[q, z], z_send.at[q, s - 1], z_recv.at[q, s - 1], at_z(s))
                for s in by_distance(nz)
            ]
        )

    def y_gather(q, arrived):
        for copy in arrived:
            copy.wait_recv()
        total = by_z[q, 0]
        for s in range(1, nz):
            total += by_z[q, s]
        mine = probe_out.at[core, q, pl.ds(pl.multiple_of(x * x_rows + y * y_rows, y_rows), y_rows)]
        mine[...] = total * scale
        return sent(
            [send(mine, mine, gy_send.at[q, s - 1], gy_recv.at[q, s - 1], at_y(s)) for s in by_distance(ny)]
        )

    def x_gather(q, arrived):
        for copy in arrived:
            copy.wait_recv()
        mine = probe_out.at[core, q, x_lines()]
        copies = sent([send(mine, mine, gx_send.at[q, s - 1], gx_recv.at[q, s - 1], at_x(s)) for s in by_distance(nx)])
        to_core = sent([send(mine, mine, gc_send.at[q, 0], gc_recv.at[q, 0], sibling)])
        return copies, to_core

    def core_gather(q, arrived):
        copies, to_core = arrived
        steps = by_distance(nx)
        for s, copy in sorted(zip(steps, copies), key=lambda pair: min(pair[0], nx - pair[0])):
            copy.wait_recv()
            piece = probe_out.at[core, q, x_lines(nx - s)]
            to_core += sent([send(piece, piece, gc_send.at[q, s], gc_recv.at[q, s], sibling)])
        return to_core

    units = [(chunk, slot) for chunk in range(CHUNKS) for slot in range(slots)]
    back_columns(*units[0])
    for this, following in zip(units, units[1:] + [None]):
        if following:
            back_columns(*following)
        back_rows(*this)
        if this == (0, slots - 1):
            front = core_scatter(0)
        if this == (1, slots // 2):
            front = x_scatter(0, front)
    back = core_scatter(1)
    place(0)
    back = x_scatter(1, back)
    front = y_scatter(0, front)
    for slot in range(1, max(2, slots // 2)):
        place(slot)
    back = y_scatter(1, back)
    front = z_gather(0, front)
    for slot in range(max(2, slots // 2), slots):
        place(slot)
    grad_copies = [
        send(grads.at[:, second, second], from_grad.at[0], grad_send.at[0], grad_recv.at[0], (down, right)),
        send(grads.at[:, first, second], from_grad.at[2], grad_send.at[2], grad_recv.at[2], (region, right)),
        send(grads.at[:, second, first], from_grad.at[1], grad_send.at[1], grad_recv.at[1], (down, pos)),
    ]
    back = z_gather(1, back)
    front = y_gather(0, front)
    back = y_gather(1, back)
    front = x_gather(0, front)
    for copy in grad_copies:
        copy.wait()
    total = grads[:, first, first]
    total += jnp.where(pos > 0, from_grad[2], 0.0)
    total += jnp.where(region > 0, from_grad[1], 0.0)
    total += jnp.where(jnp.logical_and(region > 0, pos > 0), from_grad[0], 0.0)
    obj_out[...] = total
    back = x_gather(1, back)
    front = core_gather(0, front)
    back = core_gather(1, back)
    for copy in front + back:
        copy.wait_recv()
    for copy in pending:
        copy.wait_send()


def finish(obj_in, probe_in, obj_out, probe_out, sems):
    copies = [
        pltpu.make_async_copy(probe_in, probe_out, sems.at[0]),
        pltpu.make_async_copy(obj_in, obj_out, sems.at[1]),
    ]
    for copy in copies:
        copy.start()
    for copy in copies:
        copy.wait()


def solution(mesh):
    n_region, n_pos = mesh.shape["region"], mesh.shape["pos"]
    nz = n_region // 2
    nx = 4 if n_pos == 32 else 2
    ny = n_pos // nx

    def on_device(object_tiles, probe, amplitudes, offsets, counts):
        modes, edge = probe.shape[1], probe.shape[2]
        slots = amplitudes.shape[1]
        rows = modes // CHUNKS * edge
        x_rows, y_rows = rows // nx, rows // nx // ny
        scale = 1.0 / math.sqrt(n_region * n_pos * slots)
        dma = pltpu.SemaphoreType.DMA
        any_space = pl.BlockSpec(memory_space=pl.ANY)
        vmem_space = pl.BlockSpec(memory_space=pltpu.VMEM)
        sizes = (nx, ny, nz, slots, modes, edge)
        phase_sems = []
        for count in (0, nx - 1, ny - 1, nz - 1, ny - 1, nx - 1, nx):
            shape = (CHUNKS, count) if count else (CHUNKS,)
            phase_sems += [dma(shape), dma(shape)]
        held = pl.pallas_call(
            functools.partial(kernel, sizes, scale),
            out_shape=(pltpu.VMEM((2, edge, edge), F32), pltpu.VMEM((2, CHUNKS, rows, edge), F32)),
            in_specs=[any_space] * 4 + [pl.BlockSpec(memory_space=pltpu.HBM), any_space],
            out_specs=(vmem_space, vmem_space),
            scratch_shapes=[
                pltpu.SMEM((1, 2, slots), jnp.int32),
                pltpu.SMEM((1, 1), jnp.int32),
                pltpu.VMEM((2, 2 * edge, 2 * edge), BF16),
                pltpu.VMEM((2, modes, edge, edge), F32),
                pltpu.VMEM((1, slots, edge, edge), F32),
                pltpu.VMEM((2, 2, 2 * edge, 2 * edge), BF16),
                pltpu.VMEM((slots, 2, edge, edge), F32),
                pltpu.VMEM((slots, modes, 2 * edge, edge), BF16),
                pltpu.VMEM((slots, modes, 2 * edge, edge), BF16),
                pltpu.VMEM((slots, CHUNKS, rows, 2 * edge), F32),
                pltpu.VMEM((2, 2 * edge, 2 * edge), F32),
                pltpu.VMEM((2, CHUNKS, rows, edge), F32),
                pltpu.VMEM((CHUNKS, rows, edge), F32),
                pltpu.VMEM((CHUNKS, rows, edge), F32),
                pltpu.VMEM((CHUNKS, x_rows, edge), F32),
                pltpu.VMEM((CHUNKS, nx - 1, x_rows, edge), F32),
                pltpu.VMEM((CHUNKS, ny - 1, y_rows, edge), F32),
                pltpu.VMEM((CHUNKS, nz, y_rows, edge), F32),
                pltpu.VMEM((3, 2, edge, edge), F32),
                dma((6,)), dma((3,)), dma((3,)), dma((3,)), dma((3,)),
                *phase_sems,
            ],
            compiler_params=pltpu.CompilerParams(collective_id=0, has_side_effects=True),
        )(object_tiles, probe, amplitudes, offsets, counts, jnp.asarray(dft_parts(edge)))
        obj_grad, probe_grad = pl.pallas_call(
            finish,
            out_shape=(
                jax.ShapeDtypeStruct((2, edge, edge), F32),
                jax.ShapeDtypeStruct((2, CHUNKS, rows, edge), F32),
            ),
            in_specs=[vmem_space] * 2,
            out_specs=(any_space, any_space),
            scratch_shapes=[dma((2,))],
        )(*[pltpu.with_memory_space_constraint(v, pltpu.VMEM) for v in held])
        return obj_grad, probe_grad.reshape(2, modes, edge, edge)

    return jax.shard_map(
        on_device,
        mesh=mesh,
        in_specs=(
            P(None, "region", "pos"),
            P(),
            P("region", "pos", None, None),
            P("region", None, "pos"),
            P("region", "pos"),
        ),
        out_specs=(P(None, "region", "pos"), P()),
        check_vma=False,
    )
```

```python
import functools
import math

import jax
import jax.numpy as jnp
import numpy as np
from jax import lax
from jax.experimental import pallas as pl
from jax.experimental.pallas import tpu as pltpu
from jax.sharding import PartitionSpec as P

MESH = pl.DeviceIdType.MESH
F32 = jnp.float32
BF16 = jnp.bfloat16
CHUNKS = 2
GROUP = 4


def two_parts(table):
    high = table.astype(np.float32).astype(jnp.bfloat16)
    return high, (table - high.astype(np.float64)).astype(np.float32).astype(jnp.bfloat16)


def dft_parts(order):
    index = np.arange(order)
    angle = (index[:, None] * index[None, :] % order) * (2.0 * math.pi / order)
    cos, sin = np.cos(angle) / math.sqrt(order), np.sin(angle) / math.sqrt(order)
    right = np.block([[cos, -sin], [sin, cos]])
    tables = [part for table in (right, right.T) for part in two_parts(table)]
    for start in (0, 1):
        c, s = cos[start::2, : order // 2], sin[start::2, : order // 2]
        left = np.block([[c, s], [-s, c]])
        for table in (left, left.T):
            high, low = two_parts(table)
            tables.append(np.block([[high, high], [low, low]]))
    return np.stack(tables)


def split(value):
    high = value.astype(BF16)
    return high, (value - high.astype(F32)).astype(BF16)


def dot(a, b):
    return jnp.dot(a, b, preferred_element_type=F32)


def on_left(table, value):
    both = dot(table[...], jnp.concatenate(value, axis=0))
    rows = both.shape[0] // 2
    return both[:rows] + both[rows:]


def on_right(value, tables, at):
    high, low = value
    return dot(
        jnp.concatenate([high, low, high], axis=1),
        jnp.concatenate([tables[at], tables[at], tables[at + 1]], axis=0),
    )


def one_hot(shape, dim, shift, limit=None):
    along = lax.broadcasted_iota(jnp.int32, shape, dim)
    other = lax.broadcasted_iota(jnp.int32, shape, 1 - dim)
    hit = along == other + shift
    if limit is not None:
        hit = jnp.logical_and(hit, along < limit)
    return jnp.where(hit, 1.0, 0.0).astype(BF16)


def by_distance(count):
    return sorted(range(1, count), key=lambda step: -min(step, count - step))


def kernel(
    sizes, scale, tile, probe_h, amp_h, offsets_h, counts_h, tables_h, obj_out, probe_out,
    offsets, counts, window, probe, amp, tables, crops, res_high, res_low, backs, grads, terms, own, from_core, by_x,
    from_x, from_y, by_z, from_grad, load_sem, halo_send, halo_recv, grad_send, grad_recv, core_send, core_recv,
    x_send, x_recv, y_send, y_recv, z_send, z_recv, gy_send, gy_recv, gx_send, gx_recv, gc_send, gc_recv,
):
    nx, ny, nz, slots, modes, edge = sizes
    region, pos = lax.axis_index("region"), lax.axis_index("pos")
    n_region, n_pos = 2 * nz, nx * ny
    z, core = region // 2, lax.rem(region, 2)
    x, y = pos // ny, lax.rem(pos, ny)
    up, down = lax.rem(region + n_region - 1, n_region), lax.rem(region + 1, n_region)
    left, right = lax.rem(pos + n_pos - 1, n_pos), lax.rem(pos + 1, n_pos)
    sibling = (region + 1 - 2 * core, pos)

    def at_x(step):
        return (region, lax.rem(x + step, nx) * ny + y)

    def at_y(step):
        return (region, x * ny + lax.rem(y + step, ny))

    def at_z(step):
        return (lax.rem(z + step, nz) * 2 + core, pos)

    partners = [(down, right), (down, pos), (region, right), (up, left), (up, pos), (region, left), sibling]
    partners += [at_z(s) for s in by_distance(nz)] + [at_y(s) for s in by_distance(ny)]
    partners += [at_x(s) for s in by_distance(nx)]
    barrier = pltpu.get_barrier_semaphore()
    for partner in partners:
        pl.semaphore_signal(barrier, inc=1, device_id=partner, device_id_type=MESH)

    first, second = slice(0, edge), slice(edge, 2 * edge)
    loads = [
        pltpu.make_async_copy(offsets_h, offsets, load_sem.at[0]),
        pltpu.make_async_copy(counts_h, counts, load_sem.at[1]),
        pltpu.make_async_copy(tile, window.at[0], load_sem.at[2]),
        pltpu.make_async_copy(probe_h, probe, load_sem.at[3]),
        pltpu.make_async_copy(tables_h, tables, load_sem.at[4]),
        pltpu.make_async_copy(amp_h, amp, load_sem.at[5]),
    ]
    for load in loads:
        load.start()
    pl.semaphore_wait(barrier, len(partners))

    def send(src, dst, send_sem, recv_sem, device):
        copy = pltpu.make_async_remote_copy(
            src_ref=src, dst_ref=dst, send_sem=send_sem, recv_sem=recv_sem, device_id=device, device_id_type=MESH
        )
        copy.start()
        return copy

    loads[2].wait()
    mine = window.at[0]
    halo = [
        send(mine, window.at[3], halo_send.at[0], halo_recv.at[0], (up, left)),
        send(mine, window.at[1], halo_send.at[2], halo_recv.at[2], (region, left)),
        send(mine, window.at[2], halo_send.at[1], halo_recv.at[1], (up, pos)),
    ]
    for load in loads[:2] + loads[3:]:
        load.wait()
    for copy in halo:
        copy.wait()

    row_limit = jnp.where(region < n_region - 1, 2 * edge, edge)
    col_limit = jnp.where(pos < n_pos - 1, 2 * edge, edge)
    live = counts[0, 0]
    mid = edge // 2

    def crop_at(slot):
        row0, col0 = offsets[0, 0, slot], offsets[0, 1, slot]
        rows = one_hot((edge, 2 * edge), 1, row0, row_limit)
        cols = one_hot((2 * edge, edge), 0, col0, col_limit)
        field = jnp.concatenate(
            [jnp.concatenate([window[k, part] for part in range(2) for k in pair], axis=1) for pair in ((0, 1), (2, 3))],
            axis=0,
        )
        lines = dot(rows, field).astype(BF16)
        crop = dot(jnp.concatenate([lines[:, : 2 * edge], lines[:, 2 * edge :]], axis=0), cols)
        crops[slot, 0], crops[slot, 1] = crop[:edge], crop[edge:]

    def rows_of(slot, m):
        crop_r, crop_i = crops[slot, 0], crops[slot, 1]
        exits = []
        for n in range(m, m + GROUP):
            probe_r, probe_i = probe[0, n], probe[1, n]
            exits.append(
                jnp.concatenate([probe_r * crop_r - probe_i * crop_i, probe_r * crop_i + probe_i * crop_r], axis=1)
            )
        half = on_right(split(jnp.concatenate(exits, axis=0)), tables, 0)
        for n in range(GROUP):
            block = half[n * edge : (n + 1) * edge]
            top = jnp.concatenate([block[:mid, :edge], block[:mid, edge:]], axis=0)
            bottom = jnp.concatenate([block[mid:, :edge], block[mid:, edge:]], axis=0)
            res_high[slot, 0, m + n], res_low[slot, 0, m + n] = split(top + bottom)
            res_high[slot, 1, m + n], res_low[slot, 1, m + n] = split(top - bottom)

    def halves(slot, kind, picks):
        return [jnp.concatenate([ref[slot, kind, n] for n in picks], axis=1) for ref in (res_high, res_low)]

    def columns_of(slot, m):
        fars = [on_left(tables.at[4 + 2 * kind], halves(slot, kind, range(m, m + GROUP))) for kind in range(2)]
        return [[far[:, n * edge : (n + 1) * edge] for far in fars] for n in range(GROUP)]

    def residual(slot, fars):
        for kind in range(2):
            intensity = jnp.zeros((mid, edge), F32)
            for far in fars:
                intensity += far[kind][:mid] * far[kind][:mid] + far[kind][mid:] * far[kind][mid:]
            factor = 1.0 - amp[0, slot, pl.ds(kind, mid, stride=2)] / jnp.sqrt(intensity + 1.0)
            factor = jnp.where(slot < live, factor, 0.0)
            factor = jnp.concatenate([factor, factor], axis=0)
            for m in range(modes):
                res_high[slot, kind, m], res_low[slot, kind, m] = split(fars[m][kind] * factor)

    for slot in range(slots):
        crop_at(slot)
    for m in range(0, modes, GROUP):
        rows_of(0, m)
    for slot in range(slots):
        fars = []
        for m in range(0, modes, GROUP):
            if slot + 1 < slots:
                rows_of(slot + 1, m)
            fars += columns_of(slot, m)
        residual(slot, fars)

    per = modes // CHUNKS

    def back_columns(chunk, slot):
        picks = range(chunk * per, (chunk + 1) * per)
        even, odd = (on_left(tables.at[5 + 2 * kind], halves(slot, kind, picks)) for kind in range(2))
        for kind, half in enumerate((even + odd, even - odd)):
            for n, m in enumerate(picks):
                res_high[slot, kind, m], res_low[slot, kind, m] = split(half[:, n * edge : (n + 1) * edge])

    def back_rows(chunk, slot):
        parts = []
        for ref in (res_high, res_low):
            blocks = [ref[slot, kind, m] for m in range(chunk * per, (chunk + 1) * per) for kind in range(2)]
            parts.append(
                jnp.concatenate([jnp.concatenate([block[:mid], block[mid:]], axis=1) for block in blocks], axis=0)
            )
        back = on_right(parts, tables, 2)
        backs[slot, chunk] = back
        crop_r, crop_i = crops[slot, 0], crops[slot, 1]
        for n in range(per):
            lines = slice(n * edge, (n + 1) * edge)
            back_r, back_i = back[lines, :edge], back[lines, edge:]
            term_r = crop_r * back_r + crop_i * back_i
            term_i = crop_r * back_i - crop_i * back_r
            if slot == 0:
                terms[0, chunk, lines], terms[1, chunk, lines] = term_r, term_i
            else:
                terms[0, chunk, lines] += term_r
                terms[1, chunk, lines] += term_i

    def place(slot):
        row0, col0 = offsets[0, 0, slot], offsets[0, 1, slot]
        cols = one_hot((edge, 2 * edge), 1, col0)
        rows = one_hot((2 * edge, edge), 0, row0)
        obj_r, obj_i = 0.0, 0.0
        for m in range(modes):
            lines = slice(m % per * edge, (m % per + 1) * edge)
            back_r, back_i = backs[slot, m // per, lines, first], backs[slot, m // per, lines, second]
            probe_r, probe_i = probe[0, m], probe[1, m]
            obj_r += probe_r * back_r + probe_i * back_i
            obj_i += probe_r * back_i - probe_i * back_r
        high_r, low_r = split(obj_r)
        high_i, low_i = split(obj_i)
        wide = dot(jnp.concatenate([high_r, high_i, low_r, low_i], axis=0), cols)
        wide = wide[: 2 * edge] + wide[2 * edge :]
        high, low = split(jnp.concatenate([wide[:edge], wide[edge:]], axis=1))
        field = dot(jnp.concatenate([rows, rows], axis=1), jnp.concatenate([high, low], axis=0))
        if slot == 0:
            grads[0], grads[1] = field[:, : 2 * edge], field[:, 2 * edge :]
        else:
            grads[0] += field[:, : 2 * edge]
            grads[1] += field[:, 2 * edge :]

    pending = []
    chunk_rows = per * edge
    x_rows, y_rows = chunk_rows // nx, chunk_rows // nx // ny

    def x_lines(step=0):
        return pl.ds(pl.multiple_of(lax.rem(x + step, nx) * x_rows, x_rows), x_rows)

    def y_lines(step=0):
        return pl.ds(pl.multiple_of(lax.rem(y + step, ny) * y_rows, y_rows), y_rows)

    def sent(copies):
        pending.extend(copies)
        return copies

    def core_scatter(q):
        return sent([send(terms.at[1 - core, q], from_core.at[q], core_send.at[q], core_recv.at[q], sibling)])

    def x_scatter(q, arrived):
        for copy in arrived:
            copy.wait_recv()
        own[q] = terms[core, q] + from_core[q]
        return sent(
            [
                send(own.at[q, x_lines(s)], from_x.at[q, s - 1], x_send.at[q, s - 1], x_recv.at[q, s - 1], at_x(s))
                for s in by_distance(nx)
            ]
        )

    def y_scatter(q, arrived):
        for copy in arrived:
            copy.wait_recv()
        total = own[q, x_lines()]
        for s in range(1, nx):
            total += from_x[q, s - 1]
        by_x[q] = total
        return sent(
            [
                send(by_x.at[q, y_lines(s)], from_y.at[q, s - 1], y_send.at[q, s - 1], y_recv.at[q, s - 1], at_y(s))
                for s in by_distance(ny)
            ]
        )

    def z_gather(q, arrived):
        for copy in arrived:
            copy.wait_recv()
        total = by_x[q, y_lines()]
        for s in range(1, ny):
            total += from_y[q, s - 1]
        by_z[q, z] = total
        return sent(
            [
                send(by_z.at[q, z], by_z.at[q, z], z_send.at[q, s - 1], z_recv.at[q, s - 1], at_z(s))
                for s in by_distance(nz)
            ]
        )

    def y_gather(q, arrived):
        for copy in arrived:
            copy.wait_recv()
        total = by_z[q, 0]
        for s in range(1, nz):
            total += by_z[q, s]
        mine = probe_out.at[core, q, pl.ds(pl.multiple_of(x * x_rows + y * y_rows, y_rows), y_rows)]
        mine[...] = total * scale
        return sent(
            [send(mine, mine, gy_send.at[q, s - 1], gy_recv.at[q, s - 1], at_y(s)) for s in by_distance(ny)]
        )

    def x_gather(q, arrived):
        for copy in arrived:
            copy.wait_recv()
        mine = probe_out.at[core, q, x_lines()]
        copies = sent([send(mine, mine, gx_send.at[q, s - 1], gx_recv.at[q, s - 1], at_x(s)) for s in by_distance(nx)])
        to_core = sent([send(mine, mine, gc_send.at[q, 0], gc_recv.at[q, 0], sibling)])
        return copies, to_core

    def core_gather(q, arrived):
        copies, to_core = arrived
        steps = by_distance(nx)
        for s, copy in sorted(zip(steps, copies), key=lambda pair: min(pair[0], nx - pair[0])):
            copy.wait_recv()
            piece = probe_out.at[core, q, x_lines(nx - s)]
            to_core += sent([send(piece, piece, gc_send.at[q, s], gc_recv.at[q, s], sibling)])
        return to_core

    units = [(chunk, slot) for chunk in range(CHUNKS) for slot in range(slots)]
    back_columns(*units[0])
    for this, following in zip(units, units[1:] + [None]):
        if following:
            back_columns(*following)
        back_rows(*this)
        if this == (0, slots - 1):
            front = core_scatter(0)
        if this == (1, slots // 2):
            front = x_scatter(0, front)
    back = core_scatter(1)
    place(0)
    back = x_scatter(1, back)
    front = y_scatter(0, front)
    for slot in range(1, max(2, slots // 2)):
        place(slot)
    back = y_scatter(1, back)
    front = z_gather(0, front)
    for slot in range(max(2, slots // 2), slots):
        place(slot)
    grad_copies = [
        send(grads.at[:, second, second], from_grad.at[0], grad_send.at[0], grad_recv.at[0], (down, right)),
        send(grads.at[:, first, second], from_grad.at[2], grad_send.at[2], grad_recv.at[2], (region, right)),
        send(grads.at[:, second, first], from_grad.at[1], grad_send.at[1], grad_recv.at[1], (down, pos)),
    ]
    back = z_gather(1, back)
    front = y_gather(0, front)
    back = y_gather(1, back)
    front = x_gather(0, front)
    for copy in grad_copies:
        copy.wait()
    total = grads[:, first, first]
    total += jnp.where(pos > 0, from_grad[2], 0.0)
    total += jnp.where(region > 0, from_grad[1], 0.0)
    total += jnp.where(jnp.logical_and(region > 0, pos > 0), from_grad[0], 0.0)
    obj_out[...] = total
    back = x_gather(1, back)
    for copy in pending:
        copy.wait_send()
    pending.clear()
    front = core_gather(0, front)
    back = core_gather(1, back)
    for copy in front + back:
        copy.wait_recv()
    for copy in pending:
        copy.wait_send()


def finish(obj_in, probe_in, obj_out, probe_out, sems):
    copies = [
        pltpu.make_async_copy(probe_in, probe_out, sems.at[0]),
        pltpu.make_async_copy(obj_in, obj_out, sems.at[1]),
    ]
    for copy in copies:
        copy.start()
    for copy in copies:
        copy.wait()


def solution(mesh):
    n_region, n_pos = mesh.shape["region"], mesh.shape["pos"]
    nz = n_region // 2
    nx = 4 if n_pos == 32 else 2
    ny = n_pos // nx

    def on_device(object_tiles, probe, amplitudes, offsets, counts):
        modes, edge = probe.shape[1], probe.shape[2]
        slots = amplitudes.shape[1]
        rows = modes // CHUNKS * edge
        x_rows, y_rows = rows // nx, rows // nx // ny
        scale = 1.0 / math.sqrt(n_region * n_pos * slots)
        dma = pltpu.SemaphoreType.DMA
        any_space = pl.BlockSpec(memory_space=pl.ANY)
        vmem_space = pl.BlockSpec(memory_space=pltpu.VMEM)
        sizes = (nx, ny, nz, slots, modes, edge)
        phase_sems = []
        for count in (0, nx - 1, ny - 1, nz - 1, ny - 1, nx - 1, nx):
            shape = (CHUNKS, count) if count else (CHUNKS,)
            phase_sems += [dma(shape), dma(shape)]
        held = pl.pallas_call(
            functools.partial(kernel, sizes, scale),
            out_shape=(pltpu.VMEM((2, edge, edge), F32), pltpu.VMEM((2, CHUNKS, rows, edge), F32)),
            in_specs=[any_space] * 4 + [pl.BlockSpec(memory_space=pltpu.HBM), any_space],
            out_specs=(vmem_space, vmem_space),
            scratch_shapes=[
                pltpu.SMEM((1, 2, slots), jnp.int32),
                pltpu.SMEM((1, 1), jnp.int32),
                pltpu.VMEM((4, 2, edge, edge), BF16),
                pltpu.VMEM((2, modes, edge, edge), F32),
                pltpu.VMEM((1, slots, edge, edge), F32),
                pltpu.VMEM((8, 2 * edge, 2 * edge), BF16),
                pltpu.VMEM((slots, 2, edge, edge), F32),
                pltpu.VMEM((slots, 2, modes, edge, edge), BF16),
                pltpu.VMEM((slots, 2, modes, edge, edge), BF16),
                pltpu.VMEM((slots, CHUNKS, rows, 2 * edge), F32),
                pltpu.VMEM((2, 2 * edge, 2 * edge), F32),
                pltpu.VMEM((2, CHUNKS, rows, edge), F32),
                pltpu.VMEM((CHUNKS, rows, edge), F32),
                pltpu.VMEM((CHUNKS, rows, edge), F32),
                pltpu.VMEM((CHUNKS, x_rows, edge), F32),
                pltpu.VMEM((CHUNKS, nx - 1, x_rows, edge), F32),
                pltpu.VMEM((CHUNKS, ny - 1, y_rows, edge), F32),
                pltpu.VMEM((CHUNKS, nz, y_rows, edge), F32),
                pltpu.VMEM((3, 2, edge, edge), F32),
                dma((6,)), dma((3,)), dma((3,)), dma((3,)), dma((3,)),
                *phase_sems,
            ],
            compiler_params=pltpu.CompilerParams(collective_id=0, has_side_effects=True),
        )(object_tiles, probe, amplitudes, offsets, counts, jnp.asarray(dft_parts(edge)))
        obj_grad, probe_grad = pl.pallas_call(
            finish,
            out_shape=(
                jax.ShapeDtypeStruct((2, edge, edge), F32),
                jax.ShapeDtypeStruct((2, CHUNKS, rows, edge), F32),
            ),
            in_specs=[vmem_space] * 2,
            out_specs=(any_space, any_space),
            scratch_shapes=[dma((2,))],
        )(*[pltpu.with_memory_space_constraint(v, pltpu.VMEM) for v in held])
        return obj_grad, probe_grad.reshape(2, modes, edge, edge)

    return jax.shard_map(
        on_device,
        mesh=mesh,
        in_specs=(
            P(None, "region", "pos"),
            P(),
            P("region", "pos", None, None),
            P("region", None, "pos"),
            P("region", "pos"),
        ),
        out_specs=(P(None, "region", "pos"), P()),
        check_vma=False,
    )
```

```python
import functools
import math

import jax
import jax.numpy as jnp
import numpy as np
from jax import lax
from jax.experimental import pallas as pl
from jax.experimental.pallas import tpu as pltpu
from jax.sharding import PartitionSpec as P

MESH = pl.DeviceIdType.MESH
F32 = jnp.float32
BF16 = jnp.bfloat16
CHUNKS = 2
GROUP = 4


def two_parts(table):
    high = table.astype(np.float32).astype(jnp.bfloat16)
    return high, (table - high.astype(np.float64)).astype(np.float32).astype(jnp.bfloat16)


def dft_parts(order):
    index = np.arange(order)
    angle = (index[:, None] * index[None, :] % order) * (2.0 * math.pi / order)
    cos, sin = np.cos(angle) / math.sqrt(order), np.sin(angle) / math.sqrt(order)
    right = np.block([[cos, -sin], [sin, cos]])
    tables = [part for table in (right, right.T) for part in two_parts(table)]
    for start in (0, 1):
        c, s = cos[start::2, : order // 2], sin[start::2, : order // 2]
        left = np.block([[c, s], [-s, c]])
        for table in (left, left.T):
            high, low = two_parts(table)
            tables.append(np.block([[high, high], [low, low]]))
    return np.stack(tables)


def split(value):
    high = value.astype(BF16)
    return high, (value - high.astype(F32)).astype(BF16)


def dot(a, b):
    return jnp.dot(a, b, preferred_element_type=F32)


def on_left(table, value):
    both = dot(table[...], jnp.concatenate(value, axis=0))
    rows = both.shape[0] // 2
    return both[:rows] + both[rows:]


def on_right(value, tables, at):
    high, low = value
    return dot(
        jnp.concatenate([high, low, high], axis=1),
        jnp.concatenate([tables[at], tables[at], tables[at + 1]], axis=0),
    )


def one_hot(shape, dim, shift, limit=None):
    along = lax.broadcasted_iota(jnp.int32, shape, dim)
    other = lax.broadcasted_iota(jnp.int32, shape, 1 - dim)
    hit = along == other + shift
    if limit is not None:
        hit = jnp.logical_and(hit, along < limit)
    return jnp.where(hit, 1.0, 0.0).astype(BF16)


def by_distance(count):
    return sorted(range(1, count), key=lambda step: -min(step, count - step))


def kernel(
    sizes, scale, tile, probe_h, amp_h, offsets_h, counts_h, tables_h, obj_out, probe_out,
    offsets, counts, window, probe, amp, tables, crops, res_high, res_low, backs, grads, terms, own, from_core, by_x,
    from_x, from_y, by_z, from_grad, load_sem, halo_send, halo_recv, grad_send, grad_recv, core_send, core_recv,
    x_send, x_recv, y_send, y_recv, z_send, z_recv, gy_send, gy_recv, gx_send, gx_recv, gc_send, gc_recv,
):
    nx, ny, nz, slots, modes, edge = sizes
    region, pos = lax.axis_index("region"), lax.axis_index("pos")
    n_region, n_pos = 2 * nz, nx * ny
    z, core = region // 2, lax.rem(region, 2)
    x, y = pos // ny, lax.rem(pos, ny)
    up, down = lax.rem(region + n_region - 1, n_region), lax.rem(region + 1, n_region)
    left, right = lax.rem(pos + n_pos - 1, n_pos), lax.rem(pos + 1, n_pos)
    sibling = (region + 1 - 2 * core, pos)

    def at_x(step):
        return (region, lax.rem(x + step, nx) * ny + y)

    def at_y(step):
        return (region, x * ny + lax.rem(y + step, ny))

    def at_z(step):
        return (lax.rem(z + step, nz) * 2 + core, pos)

    partners = [(down, right), (down, pos), (region, right), (up, left), (up, pos), (region, left)]
    partners += [at_z(s) for s in by_distance(nz)] + [at_y(s) for s in by_distance(ny)]
    partners += [at_x(s) for s in by_distance(nx)]
    barrier = pltpu.get_barrier_semaphore()
    for partner in partners:
        pl.semaphore_signal(barrier, inc=1, device_id=partner, device_id_type=MESH)

    first, second = slice(0, edge), slice(edge, 2 * edge)
    loads = [
        pltpu.make_async_copy(offsets_h, offsets, load_sem.at[0]),
        pltpu.make_async_copy(counts_h, counts, load_sem.at[1]),
        pltpu.make_async_copy(tile, window.at[0], load_sem.at[2]),
        pltpu.make_async_copy(probe_h, probe, load_sem.at[3]),
        pltpu.make_async_copy(tables_h, tables, load_sem.at[4]),
        pltpu.make_async_copy(amp_h, amp, load_sem.at[5]),
    ]
    for load in loads:
        load.start()
    pl.semaphore_wait(barrier, len(partners))

    def send(src, dst, send_sem, recv_sem, device):
        copy = pltpu.make_async_remote_copy(
            src_ref=src, dst_ref=dst, send_sem=send_sem, recv_sem=recv_sem, device_id=device, device_id_type=MESH
        )
        copy.start()
        return copy

    loads[2].wait()
    mine = window.at[0]
    halo = [
        send(mine, window.at[3], halo_send.at[0], halo_recv.at[0], (up, left)),
        send(mine, window.at[1], halo_send.at[2], halo_recv.at[2], (region, left)),
        send(mine, window.at[2], halo_send.at[1], halo_recv.at[1], (up, pos)),
    ]
    for load in loads[:2] + loads[3:]:
        load.wait()
    for copy in halo:
        copy.wait()

    row_limit = jnp.where(region < n_region - 1, 2 * edge, edge)
    col_limit = jnp.where(pos < n_pos - 1, 2 * edge, edge)
    live = counts[0, 0]
    mid = edge // 2

    def crop_at(slot):
        row0, col0 = offsets[0, 0, slot], offsets[0, 1, slot]
        rows = one_hot((edge, 2 * edge), 1, row0, row_limit)
        cols = one_hot((2 * edge, edge), 0, col0, col_limit)
        field = jnp.concatenate(
            [jnp.concatenate([window[k, part] for part in range(2) for k in pair], axis=1) for pair in ((0, 1), (2, 3))],
            axis=0,
        )
        lines = dot(rows, field).astype(BF16)
        crop = dot(jnp.concatenate([lines[:, : 2 * edge], lines[:, 2 * edge :]], axis=0), cols)
        crops[slot, 0], crops[slot, 1] = crop[:edge], crop[edge:]

    def rows_of(slot, m):
        crop_r, crop_i = crops[slot, 0], crops[slot, 1]
        exits = []
        for n in range(m, m + GROUP):
            probe_r, probe_i = probe[0, n], probe[1, n]
            exits.append(
                jnp.concatenate([probe_r * crop_r - probe_i * crop_i, probe_r * crop_i + probe_i * crop_r], axis=1)
            )
        half = on_right(split(jnp.concatenate(exits, axis=0)), tables, 0)
        for n in range(GROUP):
            block = half[n * edge : (n + 1) * edge]
            top = jnp.concatenate([block[:mid, :edge], block[:mid, edge:]], axis=0)
            bottom = jnp.concatenate([block[mid:, :edge], block[mid:, edge:]], axis=0)
            res_high[slot, 0, m + n], res_low[slot, 0, m + n] = split(top + bottom)
            res_high[slot, 1, m + n], res_low[slot, 1, m + n] = split(top - bottom)

    def halves(slot, kind, picks):
        return [jnp.concatenate([ref[slot, kind, n] for n in picks], axis=1) for ref in (res_high, res_low)]

    def columns_of(slot, m):
        fars = [on_left(tables.at[4 + 2 * kind], halves(slot, kind, range(m, m + GROUP))) for kind in range(2)]
        return [[far[:, n * edge : (n + 1) * edge] for far in fars] for n in range(GROUP)]

    def residual(slot, fars):
        for kind in range(2):
            intensity = jnp.zeros((mid, edge), F32)
            for far in fars:
                intensity += far[kind][:mid] * far[kind][:mid] + far[kind][mid:] * far[kind][mid:]
            factor = 1.0 - amp[0, slot, pl.ds(kind, mid, stride=2)] / jnp.sqrt(intensity + 1.0)
            factor = jnp.where(slot < live, factor, 0.0)
            factor = jnp.concatenate([factor, factor], axis=0)
            for m in range(modes):
                res_high[slot, kind, m], res_low[slot, kind, m] = split(fars[m][kind] * factor)

    for slot in range(slots):
        crop_at(slot)
    for m in range(0, modes, GROUP):
        rows_of(0, m)
    for slot in range(slots):
        fars = []
        for m in range(0, modes, GROUP):
            if slot + 1 < slots:
                rows_of(slot + 1, m)
            fars += columns_of(slot, m)
        residual(slot, fars)

    per = modes // CHUNKS

    def back_columns(chunk, slot):
        picks = range(chunk * per, (chunk + 1) * per)
        even, odd = (on_left(tables.at[5 + 2 * kind], halves(slot, kind, picks)) for kind in range(2))
        for kind, half in enumerate((even + odd, even - odd)):
            for n, m in enumerate(picks):
                res_high[slot, kind, m], res_low[slot, kind, m] = split(half[:, n * edge : (n + 1) * edge])

    def back_rows(chunk, slot):
        parts = []
        for ref in (res_high, res_low):
            blocks = [ref[slot, kind, m] for m in range(chunk * per, (chunk + 1) * per) for kind in range(2)]
            parts.append(
                jnp.concatenate([jnp.concatenate([block[:mid], block[mid:]], axis=1) for block in blocks], axis=0)
            )
        back = on_right(parts, tables, 2)
        backs[slot, chunk] = back
        crop_r, crop_i = crops[slot, 0], crops[slot, 1]
        for n in range(per):
            lines = slice(n * edge, (n + 1) * edge)
            back_r, back_i = back[lines, :edge], back[lines, edge:]
            term_r = crop_r * back_r + crop_i * back_i
            term_i = crop_r * back_i - crop_i * back_r
            if slot == 0:
                terms[0, chunk, lines], terms[1, chunk, lines] = term_r, term_i
            else:
                terms[0, chunk, lines] += term_r
                terms[1, chunk, lines] += term_i

    def place(slot):
        row0, col0 = offsets[0, 0, slot], offsets[0, 1, slot]
        cols = one_hot((edge, 2 * edge), 1, col0)
        rows = one_hot((2 * edge, edge), 0, row0)
        obj_r, obj_i = 0.0, 0.0
        for m in range(modes):
            lines = slice(m % per * edge, (m % per + 1) * edge)
            back_r, back_i = backs[slot, m // per, lines, first], backs[slot, m // per, lines, second]
            probe_r, probe_i = probe[0, m], probe[1, m]
            obj_r += probe_r * back_r + probe_i * back_i
            obj_i += probe_r * back_i - probe_i * back_r
        high_r, low_r = split(obj_r)
        high_i, low_i = split(obj_i)
        wide = dot(jnp.concatenate([high_r, high_i, low_r, low_i], axis=0), cols)
        wide = wide[: 2 * edge] + wide[2 * edge :]
        high, low = split(jnp.concatenate([wide[:edge], wide[edge:]], axis=1))
        field = dot(jnp.concatenate([rows, rows], axis=1), jnp.concatenate([high, low], axis=0))
        if slot == 0:
            grads[0], grads[1] = field[:, : 2 * edge], field[:, 2 * edge :]
        else:
            grads[0] += field[:, : 2 * edge]
            grads[1] += field[:, 2 * edge :]

    pending = []
    chunk_rows = per * edge
    x_rows, y_rows = chunk_rows // nx, chunk_rows // nx // ny

    def x_lines(step=0):
        return pl.ds(pl.multiple_of(lax.rem(x + step, nx) * x_rows, x_rows), x_rows)

    def y_lines(step=0):
        return pl.ds(pl.multiple_of(lax.rem(y + step, ny) * y_rows, y_rows), y_rows)

    def sent(copies):
        pending.extend(copies)
        return copies

    def core_scatter(q):
        return sent([send(terms.at[1 - core, q], from_core.at[q], core_send.at[q], core_recv.at[q], sibling)])

    def x_scatter(q, arrived):
        for copy in arrived:
            copy.wait_recv()
        own[q] = terms[core, q] + from_core[q]
        return sent(
            [
                send(own.at[q, x_lines(s)], from_x.at[q, s - 1], x_send.at[q, s - 1], x_recv.at[q, s - 1], at_x(s))
                for s in by_distance(nx)
            ]
        )

    def y_scatter(q, arrived):
        for copy in arrived:
            copy.wait_recv()
        total = own[q, x_lines()]
        for s in range(1, nx):
            total += from_x[q, s - 1]
        by_x[q] = total
        return sent(
            [
                send(by_x.at[q, y_lines(s)], from_y.at[q, s - 1], y_send.at[q, s - 1], y_recv.at[q, s - 1], at_y(s))
                for s in by_distance(ny)
            ]
        )

    def z_gather(q, arrived):
        for copy in arrived:
            copy.wait_recv()
        total = by_x[q, y_lines()]
        for s in range(1, ny):
            total += from_y[q, s - 1]
        by_z[q, z] = total
        return sent(
            [
                send(by_z.at[q, z], by_z.at[q, z], z_send.at[q, s - 1], z_recv.at[q, s - 1], at_z(s))
                for s in by_distance(nz)
            ]
        )

    def y_gather(q, arrived):
        for copy in arrived:
            copy.wait_recv()
        total = by_z[q, 0]
        for s in range(1, nz):
            total += by_z[q, s]
        mine = probe_out.at[core, q, pl.ds(pl.multiple_of(x * x_rows + y * y_rows, y_rows), y_rows)]
        mine[...] = total * scale
        return sent(
            [send(mine, mine, gy_send.at[q, s - 1], gy_recv.at[q, s - 1], at_y(s)) for s in by_distance(ny)]
        )

    def x_gather(q, arrived):
        for copy in arrived:
            copy.wait_recv()
        mine = probe_out.at[core, q, x_lines()]
        copies = sent([send(mine, mine, gx_send.at[q, s - 1], gx_recv.at[q, s - 1], at_x(s)) for s in by_distance(nx)])
        to_core = sent([send(mine, mine, gc_send.at[q, 0], gc_recv.at[q, 0], sibling)])
        return copies, to_core

    def core_gather(q, arrived):
        copies, to_core = arrived
        steps = by_distance(nx)
        for s, copy in sorted(zip(steps, copies), key=lambda pair: min(pair[0], nx - pair[0])):
            copy.wait_recv()
            piece = probe_out.at[core, q, x_lines(nx - s)]
            to_core += sent([send(piece, piece, gc_send.at[q, s], gc_recv.at[q, s], sibling)])
        return to_core

    units = [(chunk, slot) for chunk in range(CHUNKS) for slot in range(slots)]
    back_columns(*units[0])
    for this, following in zip(units, units[1:] + [None]):
        if following:
            back_columns(*following)
        back_rows(*this)
        if this == (0, slots - 1):
            front = core_scatter(0)
        if this == (1, slots // 2):
            front = x_scatter(0, front)
    back = core_scatter(1)
    place(0)
    back = x_scatter(1, back)
    front = y_scatter(0, front)
    for slot in range(1, max(2, slots // 2)):
        place(slot)
    back = y_scatter(1, back)
    front = z_gather(0, front)
    for slot in range(max(2, slots // 2), slots):
        place(slot)
    grad_copies = [
        send(grads.at[:, second, second], from_grad.at[0], grad_send.at[0], grad_recv.at[0], (down, right)),
        send(grads.at[:, first, second], from_grad.at[2], grad_send.at[2], grad_recv.at[2], (region, right)),
        send(grads.at[:, second, first], from_grad.at[1], grad_send.at[1], grad_recv.at[1], (down, pos)),
    ]
    back = z_gather(1, back)
    front = y_gather(0, front)
    back = y_gather(1, back)
    front = x_gather(0, front)
    back = x_gather(1, back)
    for copy in grad_copies:
        copy.wait()
    total = grads[:, first, first]
    total += jnp.where(pos > 0, from_grad[2], 0.0)
    total += jnp.where(region > 0, from_grad[1], 0.0)
    total += jnp.where(jnp.logical_and(region > 0, pos > 0), from_grad[0], 0.0)
    obj_out[...] = total
    for copy in pending:
        copy.wait_send()
    pending.clear()
    front = core_gather(0, front)
    back = core_gather(1, back)
    for copy in front + back:
        copy.wait_recv()
    for copy in pending:
        copy.wait_send()


def finish(obj_in, probe_in, obj_out, probe_out, sems):
    copies = [
        pltpu.make_async_copy(probe_in, probe_out, sems.at[0]),
        pltpu.make_async_copy(obj_in, obj_out, sems.at[1]),
    ]
    for copy in copies:
        copy.start()
    for copy in copies:
        copy.wait()


def solution(mesh):
    n_region, n_pos = mesh.shape["region"], mesh.shape["pos"]
    nz = n_region // 2
    nx = 4 if n_pos == 32 else 2
    ny = n_pos // nx

    def on_device(object_tiles, probe, amplitudes, offsets, counts):
        modes, edge = probe.shape[1], probe.shape[2]
        slots = amplitudes.shape[1]
        rows = modes // CHUNKS * edge
        x_rows, y_rows = rows // nx, rows // nx // ny
        scale = 1.0 / math.sqrt(n_region * n_pos * slots)
        dma = pltpu.SemaphoreType.DMA
        any_space = pl.BlockSpec(memory_space=pl.ANY)
        vmem_space = pl.BlockSpec(memory_space=pltpu.VMEM)
        sizes = (nx, ny, nz, slots, modes, edge)
        phase_sems = []
        for count in (0, nx - 1, ny - 1, nz - 1, ny - 1, nx - 1, nx):
            shape = (CHUNKS, count) if count else (CHUNKS,)
            phase_sems += [dma(shape), dma(shape)]
        held = pl.pallas_call(
            functools.partial(kernel, sizes, scale),
            out_shape=(pltpu.VMEM((2, edge, edge), F32), pltpu.VMEM((2, CHUNKS, rows, edge), F32)),
            in_specs=[any_space] * 4 + [pl.BlockSpec(memory_space=pltpu.HBM), any_space],
            out_specs=(vmem_space, vmem_space),
            scratch_shapes=[
                pltpu.SMEM((1, 2, slots), jnp.int32),
                pltpu.SMEM((1, 1), jnp.int32),
                pltpu.VMEM((4, 2, edge, edge), BF16),
                pltpu.VMEM((2, modes, edge, edge), F32),
                pltpu.VMEM((1, slots, edge, edge), F32),
                pltpu.VMEM((8, 2 * edge, 2 * edge), BF16),
                pltpu.VMEM((slots, 2, edge, edge), F32),
                pltpu.VMEM((slots, 2, modes, edge, edge), BF16),
                pltpu.VMEM((slots, 2, modes, edge, edge), BF16),
                pltpu.VMEM((slots, CHUNKS, rows, 2 * edge), F32),
                pltpu.VMEM((2, 2 * edge, 2 * edge), F32),
                pltpu.VMEM((2, CHUNKS, rows, edge), F32),
                pltpu.VMEM((CHUNKS, rows, edge), F32),
                pltpu.VMEM((CHUNKS, rows, edge), F32),
                pltpu.VMEM((CHUNKS, x_rows, edge), F32),
                pltpu.VMEM((CHUNKS, nx - 1, x_rows, edge), F32),
                pltpu.VMEM((CHUNKS, ny - 1, y_rows, edge), F32),
                pltpu.VMEM((CHUNKS, nz, y_rows, edge), F32),
                pltpu.VMEM((3, 2, edge, edge), F32),
                dma((6,)), dma((3,)), dma((3,)), dma((3,)), dma((3,)),
                *phase_sems,
            ],
            compiler_params=pltpu.CompilerParams(collective_id=0, has_side_effects=True),
        )(object_tiles, probe, amplitudes, offsets, counts, jnp.asarray(dft_parts(edge)))
        obj_grad, probe_grad = pl.pallas_call(
            finish,
            out_shape=(
                jax.ShapeDtypeStruct((2, edge, edge), F32),
                jax.ShapeDtypeStruct((2, CHUNKS, rows, edge), F32),
            ),
            in_specs=[vmem_space] * 2,
            out_specs=(any_space, any_space),
            scratch_shapes=[dma((2,))],
        )(*[pltpu.with_memory_space_constraint(v, pltpu.VMEM) for v in held])
        return obj_grad, probe_grad.reshape(2, modes, edge, edge)

    return jax.shard_map(
        on_device,
        mesh=mesh,
        in_specs=(
            P(None, "region", "pos"),
            P(),
            P("region", "pos", None, None),
            P("region", None, "pos"),
            P("region", "pos"),
        ),
        out_specs=(P(None, "region", "pos"), P()),
        check_vma=False,
    )
```
